256 devices in a mesh: ctx: 32 (over x, z), head: 8 (over y, core).
Axes of the slice: x: 4, y: 4, z: 8, core: 2. Of those that a mesh axis runs over, the one named last changes fastest.
Arguments:
- queries: float32 [32768, 768], P(('ctx', 'head')), may hold values from -280 to 280, as said below
- keys: float32 [32768, 768], P(('ctx', 'head')), may hold values from -7 to 7, as said below
- values: float32 [32768, 768], P(('ctx', 'head')), may hold values from -6 to 6
- grad_out: float32 [32768, 768], P(('ctx', 'head')), may hold values from -6 to 6
- neighbours: int32 [256, 2], replicated, may hold values from 0 to 255, as said below
- bias_index: int32 [256, 3], P('ctx'), may hold values from 0 to 15
- bias_table: float32 [16, 128, 128], replicated, may hold values from -6 to 6
- head_gain: float32 [16], P('head'), may hold values from 0.5 to 2
Outputs:
- attended: float32 [32768, 768], P(('ctx', 'head'))
- grad_queries: float32 [32768, 768], P(('ctx', 'head'))
- grad_keys: float32 [32768, 768], P(('ctx', 'head'))
- grad_values: float32 [32768, 768], P(('ctx', 'head'))
- grad_table: float32 [16, 128, 128], replicated
- grad_gain: float32 [16], P('head')
The draws below stay inside these ranges and needn't reach their ends.
Inputs may be any that keep to these rules, and one draw needn't show every extreme that they name: `neighbours`: each entry names a block of another ctx shard (entry // 8 differs from the query block's b // 8). Among the rows of one ctx shard, at most 1 entries name blocks of one other shard, and at most 1 distinct blocks of it; both bounds are reached in every draw. `queries`: entries have magnitude at most 280. `keys`: entries have magnitude at most 7.
All inputs are finite; a program needn't handle non-finite values.
Results may differ from the reference program's by a relative error of at most 0.0003.
Values sent between devices are 32-bit elements; how exact they have to be, the bound alone decides.
A program may use at most 128 MiB of HBM per device.

```python
import math
import jax
import jax.numpy as jnp
from jax import lax

D = 768
H = 16
BLOCK = 128
NEI = 2
NBIAS = 16
BLK_DEV = 8
NBLK = 256
NODES = 32768
CAP = 1
UCAP = 1


def normal_keys(key):
    return jnp.clip(jax.random.normal(jax.random.fold_in(key, 11), (NODES, D), jnp.float32), -6.0, 6.0)


def draw_keys(key, part):
    result = normal_keys(key)
    return result.astype(jnp.float32)


def draw_queries(key, part):
    result = jnp.clip(jax.random.normal(jax.random.fold_in(key, 12), (NODES, D), jnp.float32), -6.0, 6.0)
    return result.astype(jnp.float32)


def draw_neighbours(key, part):
    shards = NBLK // BLK_DEV
    requests = BLK_DEV * NEI
    groups = (requests + CAP - 1) // CAP

    def one_shard(position):
        shard_key = jax.random.fold_in(key, position)
        shuffled = jax.random.permutation(jax.random.fold_in(shard_key, 1), requests)
        group_of = shuffled // CAP
        place_in = shuffled % CAP
        offsets = 1 + jax.random.permutation(jax.random.fold_in(shard_key, 2), shards - 1)
        owners = (position + offsets[group_of]) % shards

        def group_pick(group_id):
            return jax.random.permutation(jax.random.fold_in(shard_key, 100 + group_id), BLK_DEV)
        candidates = jax.vmap(group_pick)(jnp.arange(groups, dtype=jnp.int32))
        local_ids = candidates[group_of, place_in % UCAP]
        return (owners * BLK_DEV + local_ids).astype(jnp.int32)
    table = jax.vmap(one_shard)(jnp.arange(shards, dtype=jnp.int32))
    return table.reshape(NBLK, NEI).astype(jnp.int32)


def set_ends(values, rng, low, high):
    longest = values.shape.index(max(values.shape))
    spots = []
    for shift in (0, 1):
        where = [jax.random.randint(jax.random.fold_in(rng, axis), (), 0, length) for axis, length in enumerate(values.shape)]
        where[longest] = (where[longest] + shift) % values.shape[longest]
        spots.append(tuple(where))
    return values.at[spots[0]].set(low).at[spots[1]].set(high)


def block_levels(stream_key, extent, pieces, least, high):
    loudness = 1.0
    for dim, parts in pieces:
        steps = jax.random.uniform(jax.random.fold_in(jax.random.fold_in(stream_key, 6), dim), (parts,), jnp.float32, least / len(pieces), high / len(pieces))
        loudness = loudness * jnp.repeat(jnp.exp(steps), extent[dim] // parts).reshape((-1,) + (1,) * (len(extent) - 1 - dim))
    return loudness


def scatter_about(key, extent, spread, reach, split=(), held_as=jnp.bfloat16):
    values = jax.random.normal(key, extent, jnp.float32) * spread
    if len(split) > 0:
        values = block_levels(key, extent, split, -0.22, 0.18) * values
    return jnp.clip(values, min=-reach, max=reach).astype(held_as)


def setup_inputs(seed: int = 0) -> dict:
    key_of = jax.random.split(jax.random.key(seed), 9)
    return {
        "queries": draw_queries(jax.random.fold_in(key_of[8], 71), 0),
        "keys": draw_keys(jax.random.fold_in(key_of[8], 71), 0),
        "values": scatter_about(key_of[2], (NODES, D), 1.0, 6.0, ((0, 256),), jnp.float32),
        "grad_out": scatter_about(key_of[3], (NODES, D), 1.0, 6.0, ((0, 256),), jnp.float32),
        "neighbours": draw_neighbours(jax.random.fold_in(key_of[8], 71), 0),
        "bias_index": set_ends(jax.random.randint(key_of[5], (NBLK, NEI + 1), 0, NBIAS), jax.random.fold_in(key_of[5], 1), 0, NBIAS - 1).astype(jnp.int32),
        "bias_table": scatter_about(key_of[6], (NBIAS, BLOCK, BLOCK), 1.0, 6.0, (), jnp.float32),
        "head_gain": jnp.clip(jnp.exp(math.log(2.0) - 1.3862944 * jax.random.uniform(key_of[7], (H,), jnp.float32) ** block_levels(key_of[7], (H,), ((0, 8),), -0.2, 0.2)), 0.5, 2.0),
    }


def attend(query_block, key_sets, value_sets, edge_bias, head_gain):
    head_count = head_gain.shape[0]
    block_rows = query_block.shape[0]
    set_blocks = key_sets.shape[0]
    query_heads = query_block.reshape(block_rows, head_count, -1)
    key_heads = key_sets.reshape(set_blocks, block_rows, head_count, -1)
    value_heads = value_sets.reshape(set_blocks * block_rows, head_count, -1)
    factor = query_heads.shape[2] ** (-0.5)
    scores = jnp.einsum('ihd,mchd->himc', query_heads, key_heads, precision=lax.Precision.HIGHEST) * factor
    scores = scores + head_gain[:, None, None, None] * jnp.transpose(edge_bias, (1, 0, 2))[None]
    scores = scores.reshape(head_count, block_rows, set_blocks * block_rows)
    maxima = lax.stop_gradient(lax.optimization_barrier(jnp.max(scores, axis=-1, keepdims=True)))
    weights = jnp.exp(scores - maxima)
    weights = weights / lax.optimization_barrier(jnp.sum(weights, axis=-1, keepdims=True))
    result = jnp.einsum('hik,khd->ihd', weights, value_heads, precision=lax.Precision.HIGHEST)
    return result.reshape(block_rows, -1)

def reference(queries, keys, values, grad_out, neighbours, bias_index, bias_table, head_gain):
    query_blocks = queries.reshape(NBLK, BLOCK, D)
    key_blocks = keys.reshape(NBLK, BLOCK, D)
    value_blocks = values.reshape(NBLK, BLOCK, D)
    grad_blocks = grad_out.reshape(NBLK, BLOCK, D)

    def visit(totals, position):
        grad_keys, grad_values, grad_table, grad_gain = totals
        block_ids = jnp.concatenate([position[None].astype(jnp.int32), neighbours[position].astype(jnp.int32)])
        table_ids = bias_index[position].astype(jnp.int32)
        edge_bias = bias_table[table_ids]
        result, pullback = jax.vjp(attend, query_blocks[position], key_blocks[block_ids], value_blocks[block_ids], edge_bias, head_gain)
        query_grad, key_grad, value_grad, bias_grad, gain_grad = pullback(grad_blocks[position])
        grad_keys = grad_keys.at[block_ids].add(key_grad)
        grad_values = grad_values.at[block_ids].add(value_grad)
        grad_table = grad_table.at[table_ids].add(bias_grad)
        return ((grad_keys, grad_values, grad_table, grad_gain + gain_grad), (result, query_grad))
    start = (jnp.zeros((NBLK, BLOCK, D), jnp.float32), jnp.zeros((NBLK, BLOCK, D), jnp.float32), jnp.zeros((NBIAS, BLOCK, BLOCK), jnp.float32), jnp.zeros((H,), jnp.float32))
    totals, stacked = lax.scan(visit, start, jnp.arange(NBLK, dtype=jnp.int32))
    grad_keys, grad_values, grad_table, grad_gain = totals
    attended, grad_queries = stacked
    return (attended.reshape(NODES, D), grad_queries.reshape(NODES, D), grad_keys.reshape(NODES, D), grad_values.reshape(NODES, D), grad_table, grad_gain)
```

```python
import jax
import jax.numpy as jnp
from jax import lax
from jax.experimental import pallas as pl
from jax.experimental.pallas import tpu as pltpu
from jax.sharding import PartitionSpec as P

BLOCK = 128
NEI = 2
HEADS = 2
MESH = pl.DeviceIdType.MESH
HIGHEST = lax.Precision.HIGHEST


def mm(a, b, ca, cb):
    return lax.dot_general(
        a, b, (((ca,), (cb,)), ((), ())), precision=HIGHEST, preferred_element_type=jnp.float32
    )


def make_kernel(nx, nz, nh, nbias, dim):
    nc = nx * nz
    blocks = nh
    requests = blocks * NEI
    pair = 2 * dim
    width = HEADS * dim
    share = nbias // nh
    piece = share * BLOCK // nc
    factor = dim ** (-0.5)

    def kernel(
        sid, rof, weight, nbr, bidx, gain,
        q_in, k_in, v_in, g_in, table,
        o_out, dq_out, dk_out, dv_out, table_out, gain_out,
        tkv, tqd, kv, qd,
        out0, out1, arr0, arr1, ret0, ret1, back0, back1, g0, g1,
        loc, oq, oqin, dkvin, ds, gacc, tl, trs, tsum, tb, tbin, tc,
        s_kv, r_kv, s_qd, r_qd, s_x0, r_x0, s_x1, r_x1, s_b0, r_b0, s_b1, r_b1,
        s_oq, r_oq, s_dkv, r_dkv, s_ta, r_ta, s_tb, r_tb, s_tc, r_tc, s_td, r_td,
    ):
        c = lax.axis_index("ctx")
        k = lax.axis_index("head")
        x = c // nz
        z = c % nz

        def there(o):
            return ((x + o // nz) % nx) * nz + (z + o % nz) % nz

        def source(o):
            return ((x + nx - o // nz) % nx) * nz + (z + nz - o % nz) % nz

        def peer(i):
            return (k + i) % nh

        barrier = pltpu.get_barrier_semaphore()

        @pl.loop(1, nh)
        def _(i):
            pl.semaphore_signal(barrier, inc=1, device_id=(c, peer(i)), device_id_type=MESH)

        @pl.loop(1, nc)
        def _(o):
            pl.semaphore_signal(barrier, inc=1, device_id=(there(o), k), device_id_type=MESH)

        def turn(first, second, dst):
            for j in range(nh):
                if width % 8 == 0 and (j * width) // 128 == (j * width + width - 1) // 128:
                    pass
            for n, ref in enumerate((first, second)):
                full = jnp.transpose(ref[...])
                for j in range(nh):
                    for h in range(HEADS):
                        row = j * width + h * dim
                        dst[j, h, n * dim : (n + 1) * dim, :] = full[row : row + dim, :]

        def to_head(src, dst, ssem, rsem, i):
            return pltpu.make_async_remote_copy(
                src.at[peer(i)], dst.at[k], ssem.at[i], rsem.at[i],
                device_id=(c, peer(i)), device_id_type=MESH,
            )

        turn(k_in, v_in, tkv)
        pl.semaphore_wait(barrier, nh + nc - 2)

        @pl.loop(1, nh)
        def _(i):
            to_head(tkv, kv, s_kv, r_kv, i).start()

        turn(q_in, g_in, tqd)

        @pl.loop(1, nh)
        def _(i):
            to_head(tqd, qd, s_qd, r_qd, i).start()

        kv[k] = tkv[k]
        qd[k] = tqd[k]

        @pl.loop(1, nh)
        def _(i):
            to_head(tkv, kv, s_kv, r_kv, i).wait_recv()

        def exchange(src, dst, ssem, rsem, o):
            return pltpu.make_async_remote_copy(
                src.at[o], dst.at[o], ssem.at[o], rsem.at[o],
                device_id=(there(o), k), device_id_type=MESH,
            )

        def give_back(src, dst, ssem, rsem, o):
            return pltpu.make_async_remote_copy(
                src.at[o], dst.at[o], ssem.at[o], rsem.at[o],
                device_id=(source(o), k), device_id_type=MESH,
            )

        for h, out, arr, ssem, rsem in ((0, out0, arr0, s_x0, r_x0), (1, out1, arr1, s_x1, r_x1)):

            @pl.loop(1, nc)
            def _(o):
                out[o] = kv[sid[there(o)], h]
                exchange(out, arr, ssem, rsem, o).start()

        @pl.loop(1, nh)
        def _(i):
            to_head(tqd, qd, s_qd, r_qd, i).wait_recv()

        gacc[...] = jnp.zeros_like(gacc)

        def attend(b, h, arr, g):
            gain_h = gain[h]
            qt = qd[b, h, 0:dim, :] * factor
            dot = qd[b, h, dim:pair, :]
            q = jnp.transpose(qt)
            do = jnp.transpose(dot)
            sets = [kv[b, h]]
            for m in range(NEI):
                owner = nbr[b * NEI + m] // blocks
                ox = (x + nx - owner // nz) % nx
                oz = (z + nz - owner % nz) % nz
                sets.append(arr[ox * nz + oz])
            bias = [table[bidx[b * (NEI + 1) + m]] for m in range(NEI + 1)]
            scores = [mm(q, t[0:dim], 1, 0) + gain_h * e for t, e in zip(sets, bias)]
            top = jnp.max(scores[0], axis=1, keepdims=True)
            for s in scores[1:]:
                top = jnp.maximum(top, jnp.max(s, axis=1, keepdims=True))
            weights = [jnp.exp(s - top) for s in scores]
            total = sum(jnp.sum(w, axis=1, keepdims=True) for w in weights)
            inverse = 1.0 / total
            weights = [w * inverse for w in weights]
            wgrad = [mm(do, t[dim:pair], 1, 0) for t in sets]
            delta = sum(jnp.sum(w * d, axis=1, keepdims=True) for w, d in zip(weights, wgrad))
            sgrad = [w * (d - delta) for w, d in zip(weights, wgrad)]
            oq[b, h, 0:dim, :] = sum(mm(t[dim:pair], w, 1, 1) for t, w in zip(sets, weights))
            oq[b, h, dim:pair, :] = factor * sum(mm(t[0:dim], s, 1, 1) for t, s in zip(sets, sgrad))
            part = jnp.zeros((8, BLOCK), jnp.float32)
            for m in range(NEI + 1):
                dk = mm(qt, sgrad[m], 1, 0)
                dv = mm(dot, weights[m], 1, 0)
                if m == 0:
                    loc[b, h, 0:dim, :] = dk
                    loc[b, h, dim:pair, :] = dv
                else:
                    g[b * NEI + m - 1, 0:dim, :] = dk
                    g[b * NEI + m - 1, dim:pair, :] = dv
                scaled = gain_h * sgrad[m]
                if h == 0:
                    ds[b * (NEI + 1) + m] = scaled
                else:
                    ds[b * (NEI + 1) + m] += scaled
                prod = sgrad[m] * bias[m]
                part = part + jnp.sum(prod.reshape(BLOCK // 8, 8, BLOCK), axis=0)
            gacc[h] += part

        def send_oq(h, i):
            return pltpu.make_async_remote_copy(
                oq.at[peer(i), h], oqin.at[k, h], s_oq.at[h, i], r_oq.at[h, i],
                device_id=(c, peer(i)), device_id_type=MESH,
            )

        def send_dkv(h, i):
            return pltpu.make_async_remote_copy(
                loc.at[peer(i), h], dkvin.at[k, h], s_dkv.at[h, i], r_dkv.at[h, i],
                device_id=(c, peer(i)), device_id_type=MESH,
            )

        for h, out, arr, ssem, rsem, g, ret, back, sb, rb in (
            (0, out0, arr0, s_x0, r_x0, g0, ret0, back0, s_b0, r_b0),
            (1, out1, arr1, s_x1, r_x1, g1, ret1, back1, s_b1, r_b1),
        ):

            @pl.loop(1, nc)
            def _(o):
                exchange(out, arr, ssem, rsem, o).wait_recv()

            @pl.loop(0, blocks)
            def _(b):
                attend(b, h, arr, g)

            @pl.loop(1, nc)
            def _(o):
                ret[o] = g[rof[source(o)]]
                give_back(ret, back, sb, rb, o).start()

            @pl.loop(1, nh)
            def _(i):
                send_oq(h, i).start()

            oqin[k, h] = oq[k, h]

        @pl.loop(0, nbias)
        def _(t):
            acc = jnp.zeros((BLOCK, BLOCK), jnp.float32)
            for r in range(blocks * (NEI + 1)):
                acc = acc + ds[r] * (bidx[r] == t).astype(jnp.float32)
            tl[t] = acc

        def table_head(i):
            return pltpu.make_async_remote_copy(
                tl.at[pl.ds(peer(i) * share, share)], trs.at[k], s_ta.at[i], r_ta.at[i],
                device_id=(c, peer(i)), device_id_type=MESH,
            )

        def table_ctx(o):
            return pltpu.make_async_remote_copy(
                tb.at[there(o)], tbin.at[c], s_tb.at[o], r_tb.at[o],
                device_id=(there(o), k), device_id_type=MESH,
            )

        def table_gather(o):
            return pltpu.make_async_remote_copy(
                tc.at[c], tc.at[c], s_tc.at[o], r_tc.at[o],
                device_id=(there(o), k), device_id_type=MESH,
            )

        def table_spread(i):
            return pltpu.make_async_remote_copy(
                tsum, table_out.at[pl.ds(k * share, share)], s_td.at[i], r_td.at[i],
                device_id=(c, peer(i)), device_id_type=MESH,
            )

        @pl.loop(1, nh)
        def _(i):
            table_head(i).start()

        trs[k] = tl[pl.ds(k * share, share)]

        @pl.loop(1, nh)
        def _(i):
            table_head(i).wait_recv()

        mine = jnp.concatenate(
            [jnp.sum(gacc[h], axis=0, keepdims=True) for h in range(HEADS)]
            + [jnp.zeros((8 - HEADS, BLOCK), jnp.float32)],
            axis=0,
        )

        @pl.loop(0, share)
        def _(t):
            acc = trs[0, t]
            for i in range(1, nh):
                acc = acc + trs[i, t]
            tsum[t] = acc

        per = BLOCK // piece

        @pl.loop(0, nc)
        def _(d):
            tb[d, 0:piece, :] = tsum[d // per, pl.ds(pl.multiple_of((d % per) * piece, 8), piece), :]
            tb[d, piece : piece + 8, :] = mine

        @pl.loop(1, nc)
        def _(o):
            table_ctx(o).start()

        tbin[c] = tb[c]

        def collect(h, back):
            @pl.loop(0, blocks)
            def _(b):
                acc = loc[b, h]
                for o in range(1, nc):
                    acc = acc + back[o] * weight[there(o) * blocks + b]
                loc[b, h] = acc

            @pl.loop(1, nh)
            def _(i):
                send_dkv(h, i).start()

            dkvin[k, h] = loc[k, h]

        @pl.loop(1, nc)
        def _(o):
            give_back(ret0, back0, s_b0, r_b0, o).wait_recv()

        collect(0, back0)

        @pl.loop(1, nc)
        def _(o):
            table_ctx(o).wait_recv()

        acc = tbin[0]
        for i in range(1, nc):
            acc = acc + tbin[i]
        tc[c] = acc[0:piece]
        gain_out[...] = jnp.broadcast_to(
            jnp.sum(acc[piece : piece + 8], axis=1, keepdims=True), (8, BLOCK)
        )

        @pl.loop(1, nc)
        def _(o):
            table_gather(o).start()

        @pl.loop(1, nc)
        def _(o):
            give_back(ret1, back1, s_b1, r_b1, o).wait_recv()

        collect(1, back1)

        @pl.loop(1, nc)
        def _(o):
            table_gather(o).wait_recv()

        @pl.loop(0, nc)
        def _(d):
            tsum[d // per, pl.ds(pl.multiple_of((d % per) * piece, 8), piece), :] = tc[d]

        @pl.loop(1, nh)
        def _(i):
            table_spread(i).start()

        table_out[pl.ds(k * share, share)] = tsum[...]

        def restore(src, first, second):
            for n, ref in enumerate((first, second)):
                rows = []
                for j in range(nh):
                    for h in range(HEADS):
                        rows.append(src[j, h, n * dim : (n + 1) * dim, :])
                ref[...] = jnp.transpose(jnp.concatenate(rows, axis=0))

        for h in range(HEADS):

            @pl.loop(1, nh)
            def _(i):
                send_oq(h, i).wait_recv()

        restore(oqin, o_out, dq_out)

        for h in range(HEADS):

            @pl.loop(1, nh)
            def _(i):
                send_dkv(h, i).wait_recv()

        restore(dkvin, dk_out, dv_out)

        @pl.loop(1, nh)
        def _(i):
            to_head(tkv, kv, s_kv, r_kv, i).wait_send()
            to_head(tqd, qd, s_qd, r_qd, i).wait_send()
            table_head(i).wait_send()
            table_spread(i).wait()
            for h in range(HEADS):
                send_oq(h, i).wait_send()
                send_dkv(h, i).wait_send()

        @pl.loop(1, nc)
        def _(o):
            exchange(out0, arr0, s_x0, r_x0, o).wait_send()
            exchange(out1, arr1, s_x1, r_x1, o).wait_send()
            give_back(ret0, back0, s_b0, r_b0, o).wait_send()
            give_back(ret1, back1, s_b1, r_b1, o).wait_send()
            table_ctx(o).wait_send()
            table_gather(o).wait_send()

    def f32(*shape):
        return pltpu.VMEM(shape, jnp.float32)

    def sems(*shape):
        return pltpu.SemaphoreType.DMA(shape)

    scratch = (
        [f32(nh, HEADS, pair, BLOCK)] * 4
        + [f32(nc, pair, BLOCK)] * 8
        + [f32(requests, pair, BLOCK)] * 2
        + [f32(nh, HEADS, pair, BLOCK)] * 4
        + [f32(blocks * (NEI + 1), BLOCK, BLOCK), f32(HEADS, 8, BLOCK)]
        + [f32(nbias, BLOCK, BLOCK), f32(nh, share, BLOCK, BLOCK), f32(share, BLOCK, BLOCK)]
        + [f32(nc, piece + 8, BLOCK)] * 2
        + [f32(nc, piece, BLOCK)]
        + [sems(nh)] * 4
        + [sems(nc)] * 8
        + [sems(HEADS, nh)] * 4
        + [sems(nh)] * 2
        + [sems(nc)] * 4
        + [sems(nh)] * 2
    )
    return kernel, scratch


def solution(mesh):
    nc = mesh.shape["ctx"]
    nh = mesh.shape["head"]
    nx = 4
    nz = nc // nx

    def body(queries, keys, values, grad_out, neighbours, bias_index, bias_table, head_gain):
        rows, columns = queries.shape
        nbias = bias_table.shape[0]
        dim = columns // (nh * HEADS)
        blocks = nh
        requests = blocks * NEI
        me = lax.axis_index("ctx")
        asks = neighbours.reshape(nc, requests)
        owner = asks // blocks
        local = asks % blocks
        hit = (owner == me)[:, :, None] & (local[:, :, None] == jnp.arange(blocks)[None, None, :])
        weight = jnp.max(hit.astype(jnp.float32), axis=1)
        sid = jnp.max(jnp.where(owner == me, local, 0), axis=1)
        own = lax.dynamic_index_in_dim(asks, me, 0, keepdims=False)
        wanted = (own // blocks)[None, :] == jnp.arange(nc)[:, None]
        rof = jnp.max(jnp.where(wanted, jnp.arange(requests)[None, :], 0), axis=1)
        kernel, scratch = make_kernel(nx, nz, nh, nbias, dim)
        smem = pl.BlockSpec(memory_space=pltpu.SMEM)
        vmem = pl.BlockSpec(memory_space=pltpu.VMEM)
        wide = jax.ShapeDtypeStruct((rows, columns), jnp.float32)
        outs = pl.pallas_call(
            kernel,
            out_shape=[wide] * 4
            + [
                jax.ShapeDtypeStruct(bias_table.shape, jnp.float32),
                jax.ShapeDtypeStruct((8, BLOCK), jnp.float32),
            ],
            in_specs=[smem] * 6 + [vmem] * 5,
            out_specs=[vmem] * 6,
            scratch_shapes=scratch,
            compiler_params=pltpu.CompilerParams(
                collective_id=0, has_side_effects=True, vmem_limit_bytes=60 * 1024 * 1024
            ),
        )(
            sid, rof, weight.reshape(-1), own, bias_index.reshape(-1), head_gain,
            queries, keys, values, grad_out, bias_table,
        )
        return (*outs[:5], outs[5][:HEADS, 0])

    return jax.shard_map(
        body,
        mesh=mesh,
        in_specs=(
            P(("ctx", "head"), None),
            P(("ctx", "head"), None),
            P(("ctx", "head"), None),
            P(("ctx", "head"), None),
            P(),
            P("ctx", None),
            P(),
            P("head"),
        ),
        out_specs=(
            P(("ctx", "head"), None),
            P(("ctx", "head"), None),
            P(("ctx", "head"), None),
            P(("ctx", "head"), None),
            P(),
            P("head"),
        ),
        check_vma=False,
    )
```

```python
import jax
import jax.numpy as jnp
from jax import lax
from jax.experimental import pallas as pl
from jax.experimental.pallas import tpu as pltpu
from jax.sharding import PartitionSpec as P

BLOCK = 128
NEI = 2
HEADS = 2
MESH = pl.DeviceIdType.MESH
HIGHEST = lax.Precision.HIGHEST


def mm(a, b, ca, cb):
    return lax.dot_general(
        a, b, (((ca,), (cb,)), ((), ())), precision=HIGHEST, preferred_element_type=jnp.float32
    )


def make_kernel(nx, nz, nh, nbias, dim):
    nc = nx * nz
    blocks = nh
    requests = blocks * NEI
    pair = 2 * dim
    width = HEADS * dim
    share = nbias // nh
    piece = share * BLOCK // nc
    factor = dim ** (-0.5)

    def kernel(
        key, rof, nbr, bidx, gain,
        q_in, k_in, v_in, g_in, table,
        o_out, dq_out, dk_out, dv_out, table_out, gain_out,
        tkv, tqd, kv0, kv1, qd, loc, oq, oqin, dkvin,
        ds, gacc, tl, trs, tsum, tb, tbin, tc,
        s_kv, r_kv, s_qd, r_qd, s_oq, r_oq, s_dkv, r_dkv,
        s_ta, r_ta, s_tb, r_tb, s_tc, r_tc, s_td, r_td,
        s_f, r_f, r_h, s_x, r_x, s_g, r_g, r_b, s_y, r_y,
        *rest,
    ):
        kv = (kv0, kv1)
        hops = [[rest[(h * 2 + s) * 5 : (h * 2 + s) * 5 + 5] for s in range(2)] for h in range(HEADS)]
        rest = rest[HEADS * 10 :]
        backs = [[rest[(h * 2 + s) * 6 : (h * 2 + s) * 6 + 6] for s in range(2)] for h in range(HEADS)]
        rest = rest[HEADS * 12 :]
        flat = [rest[h * 5 : h * 5 + 5] for h in range(HEADS)]

        c = lax.axis_index("ctx")
        k = lax.axis_index("head")
        x = c // nz
        z = c % nz

        def at(dx, dz):
            return ((x + nx + dx) % nx) * nz + (z + nz + dz) % nz

        def peer(i):
            return (k + i) % nh

        def wants(src, dst):
            return key[src * nc + dst]

        def pick(src, dst):
            return jnp.maximum(wants(src, dst), 0)

        def is_block(src, dst, b):
            return (wants(src, dst) == b).astype(jnp.float32)

        def remote(src, dst, ssem, rsem, dev):
            return pltpu.make_async_remote_copy(
                src, dst, ssem, rsem, device_id=dev, device_id_type=MESH
            )

        barrier = pltpu.get_barrier_semaphore()

        @pl.loop(1, nh)
        def _(i):
            pl.semaphore_signal(barrier, inc=1, device_id=(c, peer(i)), device_id_type=MESH)

        near = [at(ox, 0) for ox in range(1, nx)] + [at(0, 1), at(0, -1)]
        for d in near:
            pl.semaphore_signal(barrier, inc=1, device_id=(d, k), device_id_type=MESH)

        def drain(ref, sem):
            pltpu.make_async_copy(ref, ref, sem).wait()

        def turn(first, second, dst):
            for n, ref in enumerate((first, second)):
                full = jnp.transpose(ref[...])
                for j in range(nh):
                    for h in range(HEADS):
                        row = j * width + h * dim
                        dst[j, h, n * dim : (n + 1) * dim, :] = full[row : row + dim, :]

        def to_head(src, dst, ssem, rsem, i):
            return remote(src.at[peer(i)], dst.at[k], ssem, rsem, (c, peer(i)))

        def kv_head(h, i):
            return remote(
                tkv.at[peer(i), h], kv[h].at[k], s_kv, r_kv.at[h, i], (c, peer(i))
            )

        turn(k_in, v_in, tkv)
        pl.semaphore_wait(barrier, nh - 1 + len(near))
        for h in range(HEADS):

            @pl.loop(1, nh)
            def _(i):
                kv_head(h, i).start()

        for h in range(HEADS):
            kv[h][k] = tkv[k, h]

        step = (1, -1)
        far = ((0, 1), (2, 3))

        def origin(i):
            return (k + nh - i) % nh

        def forward(h, s, stage, i):
            a1, a2, a3, a4, t3 = hops[h][s]
            src, dst = (
                (kv[h].at[origin(i)], a1.at[origin(i)]),
                (a1.at[origin(i)], a2.at[origin(i)]),
                (t3.at[pl.ds(4, 2)], a3.at[pl.ds(4, 2)]),
                (t3.at[pl.ds(0, 4)], a3.at[pl.ds(0, 4)]),
                (a3.at[pl.ds(4, 2)], a4),
            )[stage]
            rsem = r_f.at[h, s, i] if stage == 0 else r_h.at[h, s, stage - 1]
            return remote(src, dst, s_f.at[h, s], rsem, (at(0, step[s]), k))

        def across(h, src, ox, oz):
            o = ox * nz + oz
            return remote(src, flat[h][0].at[o], s_x.at[h], r_x.at[h], (at(ox, 0), k))

        def deliver(h, s, dist):
            arr, xs = flat[h][:2]
            oz = (step[s] * dist) % nz
            src = at(0, -step[s] * dist)
            buf = hops[h][s][dist - 1]
            if dist <= 2:
                for ox in range(1, nx):
                    xs[ox * nz + oz] = buf[pick(src, at(ox, 0))]
                    across(h, xs.at[ox * nz + oz], ox, oz).start()
                arr[oz] = buf[pick(src, c)]
            else:
                for n, ox in enumerate(range(nx) if dist == 3 else far[s]):
                    if ox == 0:
                        arr[oz] = buf[n]
                    else:
                        across(h, buf.at[n], ox, oz).start()

        def hop_one(h, first, last):
            @pl.loop(first, last)
            def _(i):
                kv_head(h, i).wait_recv()
                for s in range(2):
                    forward(h, s, 0, i).start()

        def hop_own(h):
            for s in range(2):
                forward(h, s, 0, 0).start()

        def row(h):
            for ox in range(1, nx):
                flat[h][1][ox * nz] = kv[h][pick(c, at(ox, 0))]
                across(h, flat[h][1].at[ox * nz], ox, 0).start()

        def hop_two(h):
            @pl.loop(0, nh)
            def _(i):
                for s in range(2):
                    forward(h, s, 0, i).wait_recv()
                    forward(h, s, 1, i).start()

            for s in range(2):
                deliver(h, s, 1)

        def hop_three(h):
            for s in range(2):

                a2, t3 = hops[h][s][1], hops[h][s][4]
                drain(a2, r_h.at[h, s, 0])
                src = at(0, -2 * step[s])
                for n, ox in enumerate(far[s]):
                    t3[nx + n] = a2[pick(src, at(ox, 2 * step[s]))]
                forward(h, s, 2, 0).start()
                for ox in range(nx):
                    t3[ox] = a2[pick(src, at(ox, step[s]))]
                forward(h, s, 3, 0).start()
            for s in range(2):
                deliver(h, s, 2)

        def hop_four(h):
            for s in range(2):
                forward(h, s, 2, 0).wait_recv()
                forward(h, s, 4, 0).start()
            for s in range(2):
                forward(h, s, 3, 0).wait_recv()
                deliver(h, s, 3)

        def hop_last(h):
            for s in range(2):
                forward(h, s, 4, 0).wait_recv()
                deliver(h, s, 4)

        hop_own(0)
        turn(q_in, g_in, tqd)
        hop_one(0, 1, nh)

        @pl.loop(1, nh)
        def _(i):
            to_head(tqd, qd, s_qd, r_qd, i).start()

        qd[k] = tqd[k]
        row(0)
        hop_two(0)
        hop_own(1)
        hop_one(1, 1, 4)
        hop_three(0)
        hop_one(1, 4, nh)
        row(1)
        hop_four(0)
        hop_two(1)
        hop_last(0)

        drain(qd.at[pl.ds(0, nh - 1)], r_qd)

        gacc[...] = jnp.zeros_like(gacc)

        def attend(b, h):
            arr, g = flat[h][0], flat[h][2]
            gain_h = gain[h]
            qt = qd[b, h, 0:dim, :] * factor
            dot = qd[b, h, dim:pair, :]
            q = jnp.transpose(qt)
            do = jnp.transpose(dot)
            sets = [kv[h][b]]
            for m in range(NEI):
                owner = nbr[b * NEI + m] // blocks
                ox = (x + nx - owner // nz) % nx
                oz = (z + nz - owner % nz) % nz
                sets.append(arr[ox * nz + oz])
            bias = [table[bidx[b * (NEI + 1) + m]] for m in range(NEI + 1)]
            scores = [mm(q, t[0:dim], 1, 0) + gain_h * e for t, e in zip(sets, bias)]
            top = jnp.max(scores[0], axis=1, keepdims=True)
            for s in scores[1:]:
                top = jnp.maximum(top, jnp.max(s, axis=1, keepdims=True))
            weights = [jnp.exp(s - top) for s in scores]
            total = sum(jnp.sum(w, axis=1, keepdims=True) for w in weights)
            inverse = 1.0 / total
            weights = [w * inverse for w in weights]
            wgrad = [mm(do, t[dim:pair], 1, 0) for t in sets]
            delta = sum(jnp.sum(w * d, axis=1, keepdims=True) for w, d in zip(weights, wgrad))
            sgrad = [w * (d - delta) for w, d in zip(weights, wgrad)]
            oq[b, h, 0:dim, :] = sum(mm(t[dim:pair], w, 1, 1) for t, w in zip(sets, weights))
            oq[b, h, dim:pair, :] = factor * sum(mm(t[0:dim], s, 1, 1) for t, s in zip(sets, sgrad))
            part = jnp.zeros((8, BLOCK), jnp.float32)
            for m in range(NEI + 1):
                dk = mm(qt, sgrad[m], 1, 0)
                dv = mm(dot, weights[m], 1, 0)
                if m == 0:
                    loc[b, h, 0:dim, :] = dk
                    loc[b, h, dim:pair, :] = dv
                else:
                    g[b * NEI + m - 1, 0:dim, :] = dk
                    g[b * NEI + m - 1, dim:pair, :] = dv
                scaled = gain_h * sgrad[m]
                if h == 0:
                    ds[b * (NEI + 1) + m] = scaled
                else:
                    ds[b * (NEI + 1) + m] += scaled
                prod = sgrad[m] * bias[m]
                part = part + jnp.sum(prod.reshape(BLOCK // 8, 8, BLOCK), axis=0)
            gacc[h] += part

        def compute(h, first, last):
            @pl.loop(first, last)
            def _(b):
                attend(b, h)

        def arrived(h):
            drain(flat[h][0].at[pl.ds(nz, nc - nz)], r_x.at[h])

        def send_oq(h, i):
            return remote(
                oq.at[peer(i), h], oqin.at[k, h], s_oq, r_oq, (c, peer(i))
            )

        def send_dkv(h, i):
            return remote(
                loc.at[peer(i), h], dkvin.at[k, h], s_dkv, r_dkv, (c, peer(i))
            )

        def aside(h, ox, oz):
            rs, xb = flat[h][3:5]
            return remote(rs.at[oz, ox], xb.at[oz, ox], s_y.at[h], r_y.at[h, oz], (at(-ox, 0), k))

        def gathered(h, oz):
            drain(flat[h][4].at[oz, pl.ds(1, nx - 1)], r_y.at[h, oz])

        def outputs(h):
            g, rs, xb = flat[h][2:5]
            for oz in (4, 3, 5, 2, 6, 1, 7, 0):
                for ox in range(1, nx):
                    rs[oz, ox] = g[rof[at(-ox, -oz)]]
                    aside(h, ox, oz).start()
                if oz > 0:
                    xb[oz, 0] = g[rof[at(0, -oz)]]

            @pl.loop(1, nh)
            def _(i):
                send_oq(h, i).start()

            oqin[k, h] = oq[k, h]

        def toward(s, dist):
            return (-step[s] * dist) % nz

        def back(h, s, stage, b):
            b4, b3, b2, b1, m2, m1 = backs[h][s]
            xb = flat[h][4]
            first = far[1 - s][0]
            src, dst = (
                (xb.at[4, pl.ds(first, 2)], b4),
                (xb.at[toward(s, 3)], b3.at[pl.ds(0, 4)]),
                (b4, b3.at[pl.ds(4, 2)]),
                (m2.at[b], b2.at[b]),
                (m1.at[b], b1.at[b]),
            )[stage]
            rsem = r_g.at[h, s, stage] if stage < 3 else r_b.at[h, s, stage - 3, b]
            return remote(src, dst, s_g.at[h, s], rsem, (at(0, step[s]), k))

        def back_start(h):
            gathered(h, 4)
            for s in range(2):
                back(h, s, 0, 0).start()
            for s in range(2):
                gathered(h, toward(s, 3))
                back(h, s, 1, 0).start()
            for s in range(2):
                back(h, s, 0, 0).wait_recv()
                back(h, s, 2, 0).start()

        def back_two(h):
            xb = flat[h][4]
            for s in range(2):
                gathered(h, toward(s, 2))
                back(h, s, 1, 0).wait_recv()
                back(h, s, 2, 0).wait_recv()

            @pl.loop(1, nh + 1)
            def _(i):
                b = peer(i)
                for s in range(2):
                    b3, m2 = backs[h][s][1], backs[h][s][4]
                    oz = toward(s, 2)
                    src = at(0, 2 * step[s])
                    acc = jnp.zeros((pair, BLOCK), jnp.float32)
                    for ox in range(nx):
                        acc = acc + xb[oz, ox] * is_block(src, at(ox, 0), b)
                        acc = acc + b3[ox] * is_block(src, at(ox, -step[s]), b)
                    for n, ox in enumerate(far[1 - s]):
                        acc = acc + b3[4 + n] * is_block(src, at(ox, -2 * step[s]), b)
                    m2[b] = acc
                    back(h, s, 3, b).start()

        def back_one(h):
            xb = flat[h][4]
            for s in range(2):
                gathered(h, toward(s, 1))

            @pl.loop(1, nh + 1)
            def _(i):
                b = peer(i)
                for s in range(2):
                    b2, m1 = backs[h][s][2], backs[h][s][5]
                    oz = toward(s, 1)
                    src = at(0, step[s])
                    back(h, s, 3, b).wait_recv()
                    acc = b2[b]
                    for ox in range(nx):
                        acc = acc + xb[oz, ox] * is_block(src, at(ox, 0), b)
                    m1[b] = acc
                    back(h, s, 4, b).start()

        def back_done(h):
            xb = flat[h][4]
            gathered(h, 0)

            def total(b):
                for s in range(2):
                    back(h, s, 4, b).wait_recv()
                acc = loc[b, h] + backs[h][0][3][b] + backs[h][1][3][b]
                for ox in range(1, nx):
                    acc = acc + xb[0, ox] * is_block(c, at(ox, 0), b)
                return acc

            @pl.loop(1, nh)
            def _(i):
                loc[peer(i), h] = total(peer(i))
                send_dkv(h, i).start()

            dkvin[k, h] = total(k)

        def table_head(i):
            return remote(
                tl.at[pl.ds(peer(i) * share, share)], trs.at[k], s_ta, r_ta, (c, peer(i))
            )

        def table_ctx(o):
            d = at(o // nz, o % nz)
            return remote(tb.at[d], tbin.at[c], s_tb, r_tb, (d, k))

        def table_gather(o):
            d = at(o // nz, o % nz)
            return remote(tc.at[c], tc.at[c], s_tc, r_tc, (d, k))

        def table_spread(i):
            return remote(
                tsum, table_out.at[pl.ds(k * share, share)], s_td, r_td, (c, peer(i))
            )

        per = BLOCK // piece

        def table_first():
            @pl.loop(0, nbias)
            def _(t):
                acc = jnp.zeros((BLOCK, BLOCK), jnp.float32)
                for r in range(blocks * (NEI + 1)):
                    acc = acc + ds[r] * (bidx[r] == t).astype(jnp.float32)
                tl[t] = acc

            @pl.loop(1, nh)
            def _(i):
                table_head(i).start()

            trs[k] = tl[pl.ds(k * share, share)]

        def table_second():
            drain(trs.at[pl.ds(0, nh - 1)], r_ta)

            mine = jnp.concatenate(
                [jnp.sum(gacc[h], axis=0, keepdims=True) for h in range(HEADS)]
                + [jnp.zeros((8 - HEADS, BLOCK), jnp.float32)],
                axis=0,
            )

            @pl.loop(0, share)
            def _(t):
                acc = trs[0, t]
                for i in range(1, nh):
                    acc = acc + trs[i, t]
                tsum[t] = acc

            @pl.loop(0, nc)
            def _(d):
                tb[d, 0:piece, :] = tsum[
                    d // per, pl.ds(pl.multiple_of((d % per) * piece, 8), piece), :
                ]
                tb[d, piece : piece + 8, :] = mine

            @pl.loop(1, nc)
            def _(o):
                table_ctx(o).start()

            tbin[c] = tb[c]

        def table_third():
            drain(tbin.at[pl.ds(0, nc - 1)], r_tb)

            acc = tbin[0]
            for i in range(1, nc):
                acc = acc + tbin[i]
            tc[c] = acc[0:piece]
            gain_out[...] = jnp.broadcast_to(
                jnp.sum(acc[piece : piece + 8], axis=1, keepdims=True), (8, BLOCK)
            )

            @pl.loop(1, nc)
            def _(o):
                table_gather(o).start()

        def table_fourth():
            drain(tc.at[pl.ds(0, nc - 1)], r_tc)

            @pl.loop(0, nc)
            def _(d):
                tsum[d // per, pl.ds(pl.multiple_of((d % per) * piece, 8), piece), :] = tc[d]

            @pl.loop(1, nh)
            def _(i):
                table_spread(i).start()

            table_out[pl.ds(k * share, share)] = tsum[...]

        def restore(src, first, second):
            for n, ref in enumerate((first, second)):
                rows = []
                for j in range(nh):
                    for h in range(HEADS):
                        rows.append(src[j, h, n * dim : (n + 1) * dim, :])
                ref[...] = jnp.transpose(jnp.concatenate(rows, axis=0))

        arrived(0)
        compute(0, 0, 3)
        hop_three(1)
        compute(0, 3, 6)
        hop_four(1)
        compute(0, 6, blocks)
        hop_last(1)
        outputs(0)
        arrived(1)
        compute(1, 0, 2)
        back_start(0)
        compute(1, 2, 4)
        back_two(0)
        compute(1, 4, 7)
        back_one(0)
        compute(1, 7, blocks)
        outputs(1)
        back_start(1)
        table_first()
        back_two(1)
        table_second()
        back_done(0)
        back_one(1)
        table_third()
        drain(oqin.at[pl.ds(0, nh - 1)], r_oq)
        restore(oqin, o_out, dq_out)
        table_fourth()
        back_done(1)
        drain(dkvin.at[pl.ds(0, nh - 1)], r_dkv)
        restore(dkvin, dk_out, dv_out)
        drain(table_out.at[pl.ds(0, nbias - share)], r_td)
        for sem in (s_kv, s_qd, s_oq, s_dkv):
            drain(oqin.at[pl.ds(0, nh - 1)], sem)
        for sem in (s_ta, s_td):
            drain(trs.at[pl.ds(0, nh - 1)], sem)
        drain(tbin.at[pl.ds(0, nc - 1)], s_tb)
        drain(tc.at[pl.ds(0, nc - 1)], s_tc)
        for h in range(HEADS):
            for sem in (s_x.at[h], s_y.at[h], s_f.at[h, 0], s_f.at[h, 1], s_g.at[h, 0], s_g.at[h, 1]):
                drain(flat[h][0].at[pl.ds(0, 3 * nz)], sem)

    def f32(*shape):
        return pltpu.VMEM(shape, jnp.float32)

    def sems(*shape):
        return pltpu.SemaphoreType.DMA(shape)

    one = pltpu.SemaphoreType.DMA
    scratch = (
        [f32(nh, HEADS, pair, BLOCK)] * 2
        + [f32(nh, pair, BLOCK)] * 2
        + [f32(nh, HEADS, pair, BLOCK)] * 5
        + [f32(blocks * (NEI + 1), BLOCK, BLOCK), f32(HEADS, 8, BLOCK)]
        + [f32(nbias, BLOCK, BLOCK), f32(nh, share, BLOCK, BLOCK), f32(share, BLOCK, BLOCK)]
        + [f32(nc, piece + 8, BLOCK)] * 2
        + [f32(nc, piece, BLOCK)]
        + [one, sems(HEADS, nh)]
        + [one] * 14
        + [sems(HEADS, 2), sems(HEADS, 2, nh), sems(HEADS, 2, 4)]
        + [sems(HEADS)] * 2
        + [sems(HEADS, 2), sems(HEADS, 2, 3), sems(HEADS, 2, 2, nh)]
        + [sems(HEADS), sems(HEADS, nz)]
        + [f32(n, pair, BLOCK) for n in (blocks, blocks, 6, 2, 6)] * (2 * HEADS)
        + [f32(n, pair, BLOCK) for n in (2, 6, blocks, blocks, blocks, blocks)] * (2 * HEADS)
        + [
            f32(nc, pair, BLOCK),
            f32(nc, pair, BLOCK),
            f32(requests, pair, BLOCK),
            f32(nz, nx, pair, BLOCK),
            f32(nz, nx, pair, BLOCK),
        ]
        * HEADS
    )
    return kernel, scratch


def solution(mesh):
    nc = mesh.shape["ctx"]
    nh = mesh.shape["head"]
    nx = 4
    nz = nc // nx

    def body(queries, keys, values, grad_out, neighbours, bias_index, bias_table, head_gain):
        rows, columns = queries.shape
        nbias = bias_table.shape[0]
        dim = columns // (nh * HEADS)
        blocks = nh
        requests = blocks * NEI
        me = lax.axis_index("ctx")
        asks = neighbours.reshape(nc, requests)
        owner = asks // blocks
        local = asks % blocks
        match = owner[None, :, :] == jnp.arange(nc)[:, None, None]
        key = jnp.max(jnp.where(match, local[None, :, :], -1), axis=2)
        own = lax.dynamic_index_in_dim(asks, me, 0, keepdims=False)
        wanted = (own // blocks)[None, :] == jnp.arange(nc)[:, None]
        rof = jnp.max(jnp.where(wanted, jnp.arange(requests)[None, :], 0), axis=1)
        kernel, scratch = make_kernel(nx, nz, nh, nbias, dim)
        smem = pl.BlockSpec(memory_space=pltpu.SMEM)
        vmem = pl.BlockSpec(memory_space=pltpu.VMEM)
        wide = jax.ShapeDtypeStruct((rows, columns), jnp.float32)
        outs = pl.pallas_call(
            kernel,
            out_shape=[wide] * 4
            + [
                jax.ShapeDtypeStruct(bias_table.shape, jnp.float32),
                jax.ShapeDtypeStruct((8, BLOCK), jnp.float32),
            ],
            in_specs=[smem] * 5 + [vmem] * 5,
            out_specs=[vmem] * 6,
            scratch_shapes=scratch,
            compiler_params=pltpu.CompilerParams(
                collective_id=0, has_side_effects=True, vmem_limit_bytes=60 * 1024 * 1024
            ),
        )(
            key.reshape(-1), rof, own, bias_index.reshape(-1), head_gain,
            queries, keys, values, grad_out, bias_table,
        )
        return (*outs[:5], outs[5][:HEADS, 0])

    return jax.shard_map(
        body,
        mesh=mesh,
        in_specs=(
            P(("ctx", "head"), None),
            P(("ctx", "head"), None),
            P(("ctx", "head"), None),
            P(("ctx", "head"), None),
            P(),
            P("ctx", None),
            P(),
            P("head"),
        ),
        out_specs=(
            P(("ctx", "head"), None),
            P(("ctx", "head"), None),
            P(("ctx", "head"), None),
            P(("ctx", "head"), None),
            P(),
            P("head"),
        ),
        check_vma=False,
    )
```

```python
import jax
import jax.numpy as jnp
from jax import lax
from jax.experimental import pallas as pl
from jax.experimental.pallas import tpu as pltpu
from jax.sharding import PartitionSpec as P

BLOCK = 128
NEI = 2
HEADS = 2
MESH = pl.DeviceIdType.MESH
HIGHEST = lax.Precision.HIGHEST


def mm(a, b, ca, cb):
    return lax.dot_general(
        a, b, (((ca,), (cb,)), ((), ())), precision=HIGHEST, preferred_element_type=jnp.float32
    )


def make_kernel(nx, nz, nh, nbias, dim):
    nc = nx * nz
    blocks = nh
    requests = blocks * NEI
    pair = 2 * dim
    width = HEADS * dim
    share = nbias // nh
    piece = share * BLOCK // nc
    quarter = share * BLOCK // nx
    factor = dim ** (-0.5)

    def kernel(
        key, rof, nbr, bidx, gain,
        q_in, k_in, v_in, g_in, table,
        o_out, dq_out, dk_out, dv_out, table_out, gain_out,
        tkv, tqd, kv0, kv1, qd, loc, oq, oqin, dkvin,
        ds, gacc, tl, trs, tsum, tx, txin, tb, tbin, tc, tg,
        s_kv, r_kv, s_qd, r_qd, s_oq, r_oq, s_dkv, r_dkv,
        s_ta, r_ta, s_tx, r_tx, s_tb, r_tb, s_tc, r_tc, s_tg, r_tg, s_td, r_tm, r_td,
        s_f, r_f, r_h, s_x, r_x, s_g, r_g, r_b, s_y, r_y,
        *rest,
    ):
        kv = (kv0, kv1)
        hops = [[rest[(h * 2 + s) * 5 : (h * 2 + s) * 5 + 5] for s in range(2)] for h in range(HEADS)]
        rest = rest[HEADS * 10 :]
        backs = [[rest[(h * 2 + s) * 6 : (h * 2 + s) * 6 + 6] for s in range(2)] for h in range(HEADS)]
        rest = rest[HEADS * 12 :]
        flat = [rest[h * 5 : h * 5 + 5] for h in range(HEADS)]

        c = lax.axis_index("ctx")
        k = lax.axis_index("head")
        x = c // nz
        z = c % nz

        def at(dx, dz):
            return ((x + nx + dx) % nx) * nz + (z + nz + dz) % nz

        def peer(i):
            return (k + i) % nh

        def wants(src, dst):
            return key[src * nc + dst]

        def pick(src, dst):
            return jnp.maximum(wants(src, dst), 0)

        def is_block(src, dst, b):
            return (wants(src, dst) == b).astype(jnp.float32)

        def remote(src, dst, ssem, rsem, dev):
            return pltpu.make_async_remote_copy(
                src, dst, ssem, rsem, device_id=dev, device_id_type=MESH
            )

        barrier = pltpu.get_barrier_semaphore()

        @pl.loop(1, nh)
        def _(i):
            pl.semaphore_signal(barrier, inc=1, device_id=(c, peer(i)), device_id_type=MESH)

        near = [at(ox, 0) for ox in range(1, nx)] + [at(0, 1), at(0, -1)]
        for d in near:
            pl.semaphore_signal(barrier, inc=1, device_id=(d, k), device_id_type=MESH)

        def drain(ref, sem):
            pltpu.make_async_copy(ref, ref, sem).wait()

        def turn(first, second, dst):
            for n, ref in enumerate((first, second)):
                full = jnp.transpose(ref[...])
                for j in range(nh):
                    for h in range(HEADS):
                        row = j * width + h * dim
                        dst[j, h, n * dim : (n + 1) * dim, :] = full[row : row + dim, :]

        def to_head(src, dst, ssem, rsem, i):
            return remote(src.at[peer(i)], dst.at[k], ssem, rsem, (c, peer(i)))

        def kv_head(h, i):
            return remote(
                tkv.at[peer(i), h], kv[h].at[k], s_kv, r_kv.at[h, i], (c, peer(i))
            )

        turn(k_in, v_in, tkv)
        pl.semaphore_wait(barrier, nh - 1 + len(near))
        for h in range(HEADS):

            @pl.loop(1, nh)
            def _(i):
                kv_head(h, i).start()

        for h in range(HEADS):
            kv[h][k] = tkv[k, h]

        step = (1, -1)
        far = ((0, 1), (2, 3))

        def origin(i):
            return (k + nh - i) % nh

        def forward(h, s, stage, i):
            a1, a2, a3, a4, t3 = hops[h][s]
            src, dst = (
                (kv[h].at[origin(i)], a1.at[origin(i)]),
                (a1.at[origin(i)], a2.at[origin(i)]),
                (t3.at[pl.ds(4, 2)], a3.at[pl.ds(4, 2)]),
                (t3.at[pl.ds(0, 4)], a3.at[pl.ds(0, 4)]),
                (a3.at[pl.ds(4, 2)], a4),
            )[stage]
            rsem = r_f.at[h, s, i] if stage == 0 else r_h.at[h, s, stage - 1]
            return remote(src, dst, s_f.at[h, s], rsem, (at(0, step[s]), k))

        def across(h, src, ox, oz):
            o = ox * nz + oz
            return remote(src, flat[h][0].at[o], s_x.at[h], r_x.at[h], (at(ox, 0), k))

        def deliver(h, s, dist):
            arr, xs = flat[h][:2]
            oz = (step[s] * dist) % nz
            src = at(0, -step[s] * dist)
            buf = hops[h][s][dist - 1]
            if dist <= 2:
                for ox in range(1, nx):
                    xs[ox * nz + oz] = buf[pick(src, at(ox, 0))]
                    across(h, xs.at[ox * nz + oz], ox, oz).start()
                arr[oz] = buf[pick(src, c)]
            else:
                for n, ox in enumerate(range(nx) if dist == 3 else far[s]):
                    if ox == 0:
                        arr[oz] = buf[n]
                    else:
                        across(h, buf.at[n], ox, oz).start()

        def hop_one(h, first, last):
            @pl.loop(first, last)
            def _(i):
                kv_head(h, i).wait_recv()
                for s in range(2):
                    forward(h, s, 0, i).start()

        def hop_own(h):
            for s in range(2):
                forward(h, s, 0, 0).start()

        def row(h):
            for ox in range(1, nx):
                flat[h][1][ox * nz] = kv[h][pick(c, at(ox, 0))]
                across(h, flat[h][1].at[ox * nz], ox, 0).start()

        def hop_two(h):
            @pl.loop(0, nh)
            def _(i):
                for s in range(2):
                    forward(h, s, 0, i).wait_recv()
                    forward(h, s, 1, i).start()

            for s in range(2):
                deliver(h, s, 1)

        def hop_three(h):
            for s in range(2):

                a2, t3 = hops[h][s][1], hops[h][s][4]
                drain(a2, r_h.at[h, s, 0])
                src = at(0, -2 * step[s])
                for n, ox in enumerate(far[s]):
                    t3[nx + n] = a2[pick(src, at(ox, 2 * step[s]))]
                forward(h, s, 2, 0).start()
                for ox in range(nx):
                    t3[ox] = a2[pick(src, at(ox, step[s]))]
                forward(h, s, 3, 0).start()
            for s in range(2):
                deliver(h, s, 2)

        def hop_four(h):
            for s in range(2):
                forward(h, s, 2, 0).wait_recv()
                forward(h, s, 4, 0).start()
            for s in range(2):
                forward(h, s, 3, 0).wait_recv()
                deliver(h, s, 3)

        def hop_last(h):
            for s in range(2):
                forward(h, s, 4, 0).wait_recv()
                deliver(h, s, 4)

        hop_own(0)
        turn(q_in, g_in, tqd)
        hop_one(0, 1, nh)

        @pl.loop(1, nh)
        def _(i):
            to_head(tqd, qd, s_qd, r_qd, i).start()

        qd[k] = tqd[k]
        row(0)
        hop_two(0)
        hop_own(1)
        hop_one(1, 1, 4)
        hop_three(0)
        hop_one(1, 4, nh)
        row(1)
        hop_four(0)
        hop_two(1)
        hop_last(0)

        drain(qd.at[pl.ds(0, nh - 1)], r_qd)

        gacc[...] = jnp.zeros_like(gacc)

        def attend(b, h):
            arr, g = flat[h][0], flat[h][2]
            gain_h = gain[h]
            qt = qd[b, h, 0:dim, :] * factor
            dot = qd[b, h, dim:pair, :]
            q = jnp.transpose(qt)
            do = jnp.transpose(dot)
            sets = [kv[h][b]]
            for m in range(NEI):
                owner = nbr[b * NEI + m] // blocks
                ox = (x + nx - owner // nz) % nx
                oz = (z + nz - owner % nz) % nz
                sets.append(arr[ox * nz + oz])
            bias = [table[bidx[b * (NEI + 1) + m]] for m in range(NEI + 1)]
            scores = [mm(q, t[0:dim], 1, 0) + gain_h * e for t, e in zip(sets, bias)]
            top = jnp.max(scores[0], axis=1, keepdims=True)
            for s in scores[1:]:
                top = jnp.maximum(top, jnp.max(s, axis=1, keepdims=True))
            weights = [jnp.exp(s - top) for s in scores]
            total = sum(jnp.sum(w, axis=1, keepdims=True) for w in weights)
            inverse = 1.0 / total
            weights = [w * inverse for w in weights]
            wgrad = [mm(do, t[dim:pair], 1, 0) for t in sets]
            delta = sum(jnp.sum(w * d, axis=1, keepdims=True) for w, d in zip(weights, wgrad))
            sgrad = [w * (d - delta) for w, d in zip(weights, wgrad)]
            oq[b, h, 0:dim, :] = sum(mm(t[dim:pair], w, 1, 1) for t, w in zip(sets, weights))
            oq[b, h, dim:pair, :] = factor * sum(mm(t[0:dim], s, 1, 1) for t, s in zip(sets, sgrad))
            part = jnp.zeros((8, BLOCK), jnp.float32)
            for m in range(NEI + 1):
                dk = mm(qt, sgrad[m], 1, 0)
                dv = mm(dot, weights[m], 1, 0)
                if m == 0:
                    loc[b, h, 0:dim, :] = dk
                    loc[b, h, dim:pair, :] = dv
                else:
                    g[b * NEI + m - 1, 0:dim, :] = dk
                    g[b * NEI + m - 1, dim:pair, :] = dv
                scaled = gain_h * sgrad[m]
                if h == 0:
                    ds[b * (NEI + 1) + m] = scaled
                else:
                    ds[b * (NEI + 1) + m] += scaled
                prod = sgrad[m] * bias[m]
                part = part + jnp.sum(prod.reshape(BLOCK // 8, 8, BLOCK), axis=0)
            gacc[h] += part

        def compute(h, first, last):
            @pl.loop(first, last)
            def _(b):
                attend(b, h)

        def arrived(h):
            drain(flat[h][0].at[pl.ds(nz, nc - nz)], r_x.at[h])

        def send_oq(h, i):
            return remote(
                oq.at[peer(i), h], oqin.at[k, h], s_oq, r_oq, (c, peer(i))
            )

        def send_dkv(h, i):
            return remote(
                loc.at[peer(i), h], dkvin.at[k, h], s_dkv, r_dkv, (c, peer(i))
            )

        def aside(h, ox, oz):
            rs, xb = flat[h][3:5]
            return remote(rs.at[oz, ox], xb.at[oz, ox], s_y.at[h], r_y.at[h, oz], (at(-ox, 0), k))

        def gathered(h, oz):
            drain(flat[h][4].at[oz, pl.ds(1, nx - 1)], r_y.at[h, oz])

        def outputs(h):
            g, rs, xb = flat[h][2:5]
            for oz in (4, 3, 5, 2, 6, 1, 7, 0):
                for ox in range(1, nx):
                    rs[oz, ox] = g[rof[at(-ox, -oz)]]
                    aside(h, ox, oz).start()
                if oz > 0:
                    xb[oz, 0] = g[rof[at(0, -oz)]]

            @pl.loop(1, nh)
            def _(i):
                send_oq(h, i).start()

            oqin[k, h] = oq[k, h]

        def toward(s, dist):
            return (-step[s] * dist) % nz

        def back(h, s, stage, b):
            b4, b3, b2, b1, m2, m1 = backs[h][s]
            xb = flat[h][4]
            first = far[1 - s][0]
            src, dst = (
                (xb.at[4, pl.ds(first, 2)], b4),
                (xb.at[toward(s, 3)], b3.at[pl.ds(0, 4)]),
                (b4, b3.at[pl.ds(4, 2)]),
                (m2.at[b], b2.at[b]),
                (m1.at[b], b1.at[b]),
            )[stage]
            rsem = r_g.at[h, s, stage] if stage < 3 else r_b.at[h, s, stage - 3, b]
            return remote(src, dst, s_g.at[h, s], rsem, (at(0, step[s]), k))

        def back_start(h):
            gathered(h, 4)
            for s in range(2):
                back(h, s, 0, 0).start()
            for s in range(2):
                gathered(h, toward(s, 3))
                back(h, s, 1, 0).start()
            for s in range(2):
                back(h, s, 0, 0).wait_recv()
                back(h, s, 2, 0).start()

        def back_two(h):
            xb = flat[h][4]
            for s in range(2):
                gathered(h, toward(s, 2))
                back(h, s, 1, 0).wait_recv()
                back(h, s, 2, 0).wait_recv()

            @pl.loop(1, nh + 1)
            def _(i):
                b = peer(i)
                for s in range(2):
                    b3, m2 = backs[h][s][1], backs[h][s][4]
                    oz = toward(s, 2)
                    src = at(0, 2 * step[s])
                    acc = jnp.zeros((pair, BLOCK), jnp.float32)
                    for ox in range(nx):
                        acc = acc + xb[oz, ox] * is_block(src, at(ox, 0), b)
                        acc = acc + b3[ox] * is_block(src, at(ox, -step[s]), b)
                    for n, ox in enumerate(far[1 - s]):
                        acc = acc + b3[4 + n] * is_block(src, at(ox, -2 * step[s]), b)
                    m2[b] = acc
                    back(h, s, 3, b).start()

        def back_one(h, first=1, last=nh + 1):
            xb = flat[h][4]
            if first == 1:
                for s in range(2):
                    gathered(h, toward(s, 1))

            @pl.loop(first, last)
            def _(i):
                b = peer(i)
                for s in range(2):
                    b2, m1 = backs[h][s][2], backs[h][s][5]
                    oz = toward(s, 1)
                    src = at(0, step[s])
                    back(h, s, 3, b).wait_recv()
                    acc = b2[b]
                    for ox in range(nx):
                        acc = acc + xb[oz, ox] * is_block(src, at(ox, 0), b)
                    m1[b] = acc
                    back(h, s, 4, b).start()

        def back_done(h):
            xb = flat[h][4]
            gathered(h, 0)

            def total(b):
                for s in range(2):
                    back(h, s, 4, b).wait_recv()
                acc = loc[b, h] + backs[h][0][3][b] + backs[h][1][3][b]
                for ox in range(1, nx):
                    acc = acc + xb[0, ox] * is_block(c, at(ox, 0), b)
                return acc

            @pl.loop(1, nh)
            def _(i):
                loc[peer(i), h] = total(peer(i))
                send_dkv(h, i).start()

            dkvin[k, h] = total(k)

        def table_head(i):
            return remote(
                tl.at[pl.ds(peer(i) * share, share)], trs.at[k], s_ta, r_ta, (c, peer(i))
            )

        def table_x(ox):
            return remote(tx.at[(x + ox) % nx], txin.at[x], s_tx, r_tx, (at(ox, 0), k))

        def table_z(oz):
            return remote(tb.at[(z + oz) % nz], tbin.at[z], s_tb, r_tb, (at(0, oz), k))

        def gather_z(oz):
            return remote(tc.at[z], tc.at[z], s_tc, r_tc, (at(0, oz), k))

        def gather_x(ox):
            return remote(tg.at[x], tg.at[x], s_tg, r_tg, (at(ox, 0), k))

        mate = 2 * (k // 2) + 1 - k % 2

        def table_y(i):
            part = table_out.at[pl.ds(k * share, share)]
            return remote(tsum, part, s_td, r_td.at[i], (c, (k + 2 * i) % nh))

        def table_mate(src, j):
            return remote(src, table_out.at[pl.ds(j * share, share)], s_td, r_tm, (c, mate))

        def table_first():
            @pl.loop(0, nbias)
            def _(t):
                acc = jnp.zeros((BLOCK, BLOCK), jnp.float32)
                for r in range(blocks * (NEI + 1)):
                    acc = acc + ds[r] * (bidx[r] == t).astype(jnp.float32)
                tl[t] = acc

            @pl.loop(1, nh)
            def _(i):
                table_head(i).start()

            trs[k] = tl[pl.ds(k * share, share)]

        def table_second():
            mine = jnp.concatenate(
                [jnp.sum(gacc[h], axis=0, keepdims=True) for h in range(HEADS)]
                + [jnp.zeros((8 - HEADS, BLOCK), jnp.float32)],
                axis=0,
            )
            drain(trs.at[pl.ds(0, nh - 1)], r_ta)
            for t in range(nx):
                rows = pl.ds(t * quarter % BLOCK, quarter)
                acc = trs[0, t * quarter // BLOCK, rows, :]
                for i in range(1, nh):
                    acc = acc + trs[i, t * quarter // BLOCK, rows, :]
                tx[t, 0:quarter, :] = acc
                tx[t, quarter : quarter + 8, :] = mine
            for ox in range(1, nx):
                table_x(ox).start()
            txin[x] = tx[x]

        def table_third():
            drain(txin.at[pl.ds(0, nx - 1)], r_tx)
            acc = txin[0]
            for i in range(1, nx):
                acc = acc + txin[i]
            for t in range(nz):
                tb[t, 0:piece, :] = acc[t * piece : (t + 1) * piece]
                tb[t, piece : piece + 8, :] = acc[quarter:]
            for oz in range(1, nz):
                table_z(oz).start()
            tbin[z] = tb[z]

        def table_fourth():
            drain(tbin.at[pl.ds(0, nz - 1)], r_tb)
            acc = tbin[0]
            for i in range(1, nz):
                acc = acc + tbin[i]
            tc[z] = acc[0:piece]
            gain_out[...] = jnp.broadcast_to(
                jnp.sum(acc[piece : piece + 8], axis=1, keepdims=True), (8, BLOCK)
            )
            for oz in range(1, nz):
                gather_z(oz).start()

        def table_fifth():
            drain(tc.at[pl.ds(0, nz - 1)], r_tc)
            tg[x] = tc[...].reshape(quarter, BLOCK)
            for ox in range(1, nx):
                gather_x(ox).start()

        def table_sixth():
            drain(tg.at[pl.ds(0, nx - 1)], r_tg)
            for t in range(nx):
                tsum[t * quarter // BLOCK, pl.ds(t * quarter % BLOCK, quarter), :] = tg[t]
            for i in range(1, nh // 2):
                table_y(i).start()
            table_mate(tsum, k).start()
            table_out[pl.ds(k * share, share)] = tsum[...]

        def table_last():
            for i in range(1, nh // 2):
                j = (k + nh - 2 * i) % nh
                part = table_out.at[pl.ds(j * share, share)]
                drain(part, r_td.at[i])
                table_mate(part, j).start()

        def restore(src, first, second):
            for n, ref in enumerate((first, second)):
                rows = []
                for j in range(nh):
                    for h in range(HEADS):
                        rows.append(src[j, h, n * dim : (n + 1) * dim, :])
                ref[...] = jnp.transpose(jnp.concatenate(rows, axis=0))

        arrived(0)
        compute(0, 0, 3)
        hop_three(1)
        compute(0, 3, 6)
        hop_four(1)
        compute(0, 6, blocks)
        hop_last(1)
        outputs(0)
        arrived(1)
        compute(1, 0, 2)
        back_start(0)
        compute(1, 2, 4)
        back_two(0)
        compute(1, 4, 7)
        back_one(0)
        compute(1, 7, blocks)
        outputs(1)
        table_first()
        back_start(1)
        back_done(0)
        back_two(1)
        table_second()
        table_third()
        back_one(1, 1, 5)
        table_fourth()
        back_one(1, 5)
        table_fifth()
        table_sixth()
        drain(oqin.at[pl.ds(0, nh - 1)], r_oq)
        restore(oqin, o_out, dq_out)
        back_done(1)
        table_last()
        drain(dkvin.at[pl.ds(0, nh - 1)], r_dkv)
        restore(dkvin, dk_out, dv_out)
        drain(table_out.at[pl.ds(0, nbias // 2)], r_tm)
        for sem in (s_kv, s_qd, s_oq, s_dkv):
            drain(oqin.at[pl.ds(0, nh - 1)], sem)
        for sem in (s_ta, s_td):
            drain(trs.at[pl.ds(0, nh - 1)], sem)
        drain(txin.at[pl.ds(0, nx - 1)], s_tx)
        drain(tbin.at[pl.ds(0, nz - 1)], s_tb)
        drain(tc.at[pl.ds(0, nz - 1)], s_tc)
        drain(tg.at[pl.ds(0, nx - 1)], s_tg)
        for h in range(HEADS):
            for sem in (s_x.at[h], s_y.at[h], s_f.at[h, 0], s_f.at[h, 1], s_g.at[h, 0], s_g.at[h, 1]):
                drain(flat[h][0].at[pl.ds(0, 3 * nz)], sem)

    def f32(*shape):
        return pltpu.VMEM(shape, jnp.float32)

    def sems(*shape):
        return pltpu.SemaphoreType.DMA(shape)

    one = pltpu.SemaphoreType.DMA
    scratch = (
        [f32(nh, HEADS, pair, BLOCK)] * 2
        + [f32(nh, pair, BLOCK)] * 2
        + [f32(nh, HEADS, pair, BLOCK)] * 5
        + [f32(blocks * (NEI + 1), BLOCK, BLOCK), f32(HEADS, 8, BLOCK)]
        + [f32(nbias, BLOCK, BLOCK), f32(nh, share, BLOCK, BLOCK), f32(share, BLOCK, BLOCK)]
        + [f32(nx, quarter + 8, BLOCK)] * 2
        + [f32(nz, piece + 8, BLOCK)] * 2
        + [f32(nz, piece, BLOCK), f32(nx, quarter, BLOCK)]
        + [one, sems(HEADS, nh)]
        + [one] * 18
        + [sems(nh // 2)]
        + [sems(HEADS, 2), sems(HEADS, 2, nh), sems(HEADS, 2, 4)]
        + [sems(HEADS)] * 2
        + [sems(HEADS, 2), sems(HEADS, 2, 3), sems(HEADS, 2, 2, nh)]
        + [sems(HEADS), sems(HEADS, nz)]
        + [f32(n, pair, BLOCK) for n in (blocks, blocks, 6, 2, 6)] * (2 * HEADS)
        + [f32(n, pair, BLOCK) for n in (2, 6, blocks, blocks, blocks, blocks)] * (2 * HEADS)
        + [
            f32(nc, pair, BLOCK),
            f32(nc, pair, BLOCK),
            f32(requests, pair, BLOCK),
            f32(nz, nx, pair, BLOCK),
            f32(nz, nx, pair, BLOCK),
        ]
        * HEADS
    )
    return kernel, scratch


def solution(mesh):
    nc = mesh.shape["ctx"]
    nh = mesh.shape["head"]
    nx = 4
    nz = nc // nx

    def body(queries, keys, values, grad_out, neighbours, bias_index, bias_table, head_gain):
        rows, columns = queries.shape
        nbias = bias_table.shape[0]
        dim = columns // (nh * HEADS)
        blocks = nh
        requests = blocks * NEI
        me = lax.axis_index("ctx")
        asks = neighbours.reshape(nc, requests)
        owner = asks // blocks
        local = asks % blocks
        match = owner[None, :, :] == jnp.arange(nc)[:, None, None]
        key = jnp.max(jnp.where(match, local[None, :, :], -1), axis=2)
        own = lax.dynamic_index_in_dim(asks, me, 0, keepdims=False)
        wanted = (own // blocks)[None, :] == jnp.arange(nc)[:, None]
        rof = jnp.max(jnp.where(wanted, jnp.arange(requests)[None, :], 0), axis=1)
        kernel, scratch = make_kernel(nx, nz, nh, nbias, dim)
        smem = pl.BlockSpec(memory_space=pltpu.SMEM)
        vmem = pl.BlockSpec(memory_space=pltpu.VMEM)
        wide = jax.ShapeDtypeStruct((rows, columns), jnp.float32)
        outs = pl.pallas_call(
            kernel,
            out_shape=[wide] * 4
            + [
                jax.ShapeDtypeStruct(bias_table.shape, jnp.float32),
                jax.ShapeDtypeStruct((8, BLOCK), jnp.float32),
            ],
            in_specs=[smem] * 5 + [vmem] * 5,
            out_specs=[vmem] * 6,
            scratch_shapes=scratch,
            compiler_params=pltpu.CompilerParams(
                collective_id=0, has_side_effects=True, vmem_limit_bytes=60 * 1024 * 1024
            ),
        )(
            key.reshape(-1), rof, own, bias_index.reshape(-1), head_gain,
            queries, keys, values, grad_out, bias_table,
        )
        return (*outs[:5], outs[5][:HEADS, 0])

    return jax.shard_map(
        body,
        mesh=mesh,
        in_specs=(
            P(("ctx", "head"), None),
            P(("ctx", "head"), None),
            P(("ctx", "head"), None),
            P(("ctx", "head"), None),
            P(),
            P("ctx", None),
            P(),
            P("head"),
        ),
        out_specs=(
            P(("ctx", "head"), None),
            P(("ctx", "head"), None),
            P(("ctx", "head"), None),
            P(("ctx", "head"), None),
            P(),
            P("head"),
        ),
        check_vma=False,
    )
```

```python
import jax
import jax.numpy as jnp
from jax import lax
from jax.experimental import pallas as pl
from jax.experimental.pallas import tpu as pltpu
from jax.sharding import PartitionSpec as P

BLOCK = 128
NEI = 2
HEADS = 2
MESH = pl.DeviceIdType.MESH
HIGHEST = lax.Precision.HIGHEST


def mm(a, b, ca, cb):
    return lax.dot_general(
        a, b, (((ca,), (cb,)), ((), ())), precision=HIGHEST, preferred_element_type=jnp.float32
    )


def make_kernel(nx, nz, nh, nbias, dim):
    nc = nx * nz
    blocks = nh
    requests = blocks * NEI
    pair = 2 * dim
    width = HEADS * dim
    share = nbias // nh
    piece = share * BLOCK // nc
    quarter = share * BLOCK // nx
    factor = dim ** (-0.5)

    def kernel(
        key, rof, nbr, bidx, gain,
        q_hbm, k_hbm, v_hbm, g_hbm, table_hbm,
        o_out, dq_out, dk_out, dv_out, table_out, gain_out,
        q_in, k_in, v_in, g_in, table, s_in,
        tkv, tqd, kv0, kv1, qd, loc, oq, oqin, dkvin,
        ds, gacc, tl, trs, tsum, tx, txin, tb, tbin, tc, tg,
        s_kv, r_kv, s_qd, r_qd, s_oq, r_oq, s_dkv, r_dkv,
        s_ta, r_ta, s_tx, r_tx, s_tb, r_tb, s_tc, r_tc, s_tg, r_tg, s_td, r_tm, r_td,
        s_f, r_f, r_h, s_x, r_x, s_g, r_g, r_b, s_y, r_y,
        *rest,
    ):
        kv = (kv0, kv1)
        hops = [[rest[(h * 2 + s) * 5 : (h * 2 + s) * 5 + 5] for s in range(2)] for h in range(HEADS)]
        rest = rest[HEADS * 10 :]
        backs = [[rest[(h * 2 + s) * 6 : (h * 2 + s) * 6 + 6] for s in range(2)] for h in range(HEADS)]
        rest = rest[HEADS * 12 :]
        flat = [rest[h * 5 : h * 5 + 5] for h in range(HEADS)]

        c = lax.axis_index("ctx")
        k = lax.axis_index("head")
        x = c // nz
        z = c % nz

        def at(dx, dz):
            return ((x + nx + dx) % nx) * nz + (z + nz + dz) % nz

        def peer(i):
            return (k + i) % nh

        def wants(src, dst):
            return key[src * nc + dst]

        def pick(src, dst):
            return jnp.maximum(wants(src, dst), 0)

        def is_block(src, dst, b):
            return (wants(src, dst) == b).astype(jnp.float32)

        def remote(src, dst, ssem, rsem, dev):
            return pltpu.make_async_remote_copy(
                src, dst, ssem, rsem, device_id=dev, device_id_type=MESH
            )

        inputs = [
            pltpu.make_async_copy(src, dst, s_in.at[n])
            for n, (src, dst) in enumerate(
                (
                    (k_hbm, k_in), (v_hbm, v_in), (q_hbm, q_in), (g_hbm, g_in), (table_hbm, table)
                )
            )
        ]
        for copy in inputs:
            copy.start()

        barrier = pltpu.get_barrier_semaphore()

        @pl.loop(1, nh)
        def _(i):
            pl.semaphore_signal(barrier, inc=1, device_id=(c, peer(i)), device_id_type=MESH)

        near = [at(ox, 0) for ox in range(1, nx)] + [at(0, 1), at(0, -1)]
        for d in near:
            pl.semaphore_signal(barrier, inc=1, device_id=(d, k), device_id_type=MESH)

        def drain(ref, sem):
            pltpu.make_async_copy(ref, ref, sem).wait()

        def turn(first, second, dst):
            for n, ref in enumerate((first, second)):
                full = jnp.transpose(ref[...])
                for j in range(nh):
                    for h in range(HEADS):
                        row = j * width + h * dim
                        dst[j, h, n * dim : (n + 1) * dim, :] = full[row : row + dim, :]

        def to_head(src, dst, ssem, rsem, i):
            return remote(src.at[peer(i)], dst.at[k], ssem, rsem, (c, peer(i)))

        def kv_head(h, i):
            return remote(
                tkv.at[peer(i), h], kv[h].at[k], s_kv, r_kv.at[h, i], (c, peer(i))
            )

        inputs[0].wait()
        inputs[1].wait()
        turn(k_in, v_in, tkv)
        pl.semaphore_wait(barrier, nh - 1 + len(near))
        for h in range(HEADS):

            @pl.loop(1, nh)
            def _(i):
                kv_head(h, i).start()

        for h in range(HEADS):
            kv[h][k] = tkv[k, h]

        step = (1, -1)
        far = ((0, 1), (2, 3))

        def origin(i):
            return (k + nh - i) % nh

        def forward(h, s, stage, i):
            a1, a2, a3, a4, t3 = hops[h][s]
            src, dst = (
                (kv[h].at[origin(i)], a1.at[origin(i)]),
                (a1.at[origin(i)], a2.at[origin(i)]),
                (t3.at[pl.ds(4, 2)], a3.at[pl.ds(4, 2)]),
                (t3.at[pl.ds(0, 4)], a3.at[pl.ds(0, 4)]),
                (a3.at[pl.ds(4, 2)], a4),
            )[stage]
            rsem = r_f.at[h, s, i] if stage == 0 else r_h.at[h, s, stage - 1]
            return remote(src, dst, s_f.at[h, s], rsem, (at(0, step[s]), k))

        def across(h, src, ox, oz):
            o = ox * nz + oz
            return remote(src, flat[h][0].at[o], s_x.at[h], r_x.at[h], (at(ox, 0), k))

        def deliver(h, s, dist):
            arr, xs = flat[h][:2]
            oz = (step[s] * dist) % nz
            src = at(0, -step[s] * dist)
            buf = hops[h][s][dist - 1]
            if dist <= 2:
                for ox in range(1, nx):
                    xs[ox * nz + oz] = buf[pick(src, at(ox, 0))]
                    across(h, xs.at[ox * nz + oz], ox, oz).start()
                arr[oz] = buf[pick(src, c)]
            else:
                for n, ox in enumerate(range(nx) if dist == 3 else far[s]):
                    if ox == 0:
                        arr[oz] = buf[n]
                    else:
                        across(h, buf.at[n], ox, oz).start()

        def hop_one(h, first, last):
            @pl.loop(first, last)
            def _(i):
                kv_head(h, i).wait_recv()
                for s in range(2):
                    forward(h, s, 0, i).start()

        def hop_own(h):
            for s in range(2):
                forward(h, s, 0, 0).start()

        def row(h):
            for ox in range(1, nx):
                flat[h][1][ox * nz] = kv[h][pick(c, at(ox, 0))]
                across(h, flat[h][1].at[ox * nz], ox, 0).start()

        def hop_two(h):
            @pl.loop(0, nh)
            def _(i):
                for s in range(2):
                    forward(h, s, 0, i).wait_recv()
                    forward(h, s, 1, i).start()

            for s in range(2):
                deliver(h, s, 1)

        def hop_three(h):
            for s in range(2):

                a2, t3 = hops[h][s][1], hops[h][s][4]
                drain(a2, r_h.at[h, s, 0])
                src = at(0, -2 * step[s])
                for n, ox in enumerate(far[s]):
                    t3[nx + n] = a2[pick(src, at(ox, 2 * step[s]))]
                forward(h, s, 2, 0).start()
                for ox in range(nx):
                    t3[ox] = a2[pick(src, at(ox, step[s]))]
                forward(h, s, 3, 0).start()
            for s in range(2):
                deliver(h, s, 2)

        def hop_four(h):
            for s in range(2):
                forward(h, s, 2, 0).wait_recv()
                forward(h, s, 4, 0).start()
            for s in range(2):
                forward(h, s, 3, 0).wait_recv()
                deliver(h, s, 3)

        def hop_last(h):
            for s in range(2):
                forward(h, s, 4, 0).wait_recv()
                deliver(h, s, 4)

        hop_own(0)
        inputs[2].wait()
        inputs[3].wait()
        turn(q_in, g_in, tqd)
        hop_one(0, 1, nh)

        @pl.loop(1, nh)
        def _(i):
            to_head(tqd, qd, s_qd, r_qd, i).start()

        qd[k] = tqd[k]
        row(0)
        hop_two(0)
        hop_own(1)
        hop_one(1, 1, 4)
        hop_three(0)
        hop_one(1, 4, nh)
        row(1)
        hop_four(0)
        hop_two(1)
        hop_last(0)

        drain(qd.at[pl.ds(0, nh - 1)], r_qd)

        inputs[4].wait()
        gacc[...] = jnp.zeros_like(gacc)

        def attend(b, h):
            arr, g = flat[h][0], flat[h][2]
            gain_h = gain[h]
            qt = qd[b, h, 0:dim, :] * factor
            dot = qd[b, h, dim:pair, :]
            q = jnp.transpose(qt)
            do = jnp.transpose(dot)
            sets = [kv[h][b]]
            for m in range(NEI):
                owner = nbr[b * NEI + m] // blocks
                ox = (x + nx - owner // nz) % nx
                oz = (z + nz - owner % nz) % nz
                sets.append(arr[ox * nz + oz])
            bias = [table[bidx[b * (NEI + 1) + m]] for m in range(NEI + 1)]
            scores = [mm(q, t[0:dim], 1, 0) + gain_h * e for t, e in zip(sets, bias)]
            top = jnp.max(scores[0], axis=1, keepdims=True)
            for s in scores[1:]:
                top = jnp.maximum(top, jnp.max(s, axis=1, keepdims=True))
            weights = [jnp.exp(s - top) for s in scores]
            total = sum(jnp.sum(w, axis=1, keepdims=True) for w in weights)
            inverse = 1.0 / total
            weights = [w * inverse for w in weights]
            wgrad = [mm(do, t[dim:pair], 1, 0) for t in sets]
            delta = sum(jnp.sum(w * d, axis=1, keepdims=True) for w, d in zip(weights, wgrad))
            sgrad = [w * (d - delta) for w, d in zip(weights, wgrad)]
            oq[b, h, 0:dim, :] = sum(mm(t[dim:pair], w, 1, 1) for t, w in zip(sets, weights))
            oq[b, h, dim:pair, :] = factor * sum(mm(t[0:dim], s, 1, 1) for t, s in zip(sets, sgrad))
            part = jnp.zeros((8, BLOCK), jnp.float32)
            for m in range(NEI + 1):
                dk = mm(qt, sgrad[m], 1, 0)
                dv = mm(dot, weights[m], 1, 0)
                if m == 0:
                    loc[b, h, 0:dim, :] = dk
                    loc[b, h, dim:pair, :] = dv
                else:
                    g[b * NEI + m - 1, 0:dim, :] = dk
                    g[b * NEI + m - 1, dim:pair, :] = dv
                scaled = gain_h * sgrad[m]
                if h == 0:
                    ds[b * (NEI + 1) + m] = scaled
                else:
                    ds[b * (NEI + 1) + m] += scaled
                prod = sgrad[m] * bias[m]
                part = part + jnp.sum(prod.reshape(BLOCK // 8, 8, BLOCK), axis=0)
            gacc[h] += part

        def compute(h, first, last):
            @pl.loop(first, last)
            def _(b):
                attend(b, h)

        def arrived(h):
            drain(flat[h][0].at[pl.ds(nz, nc - nz)], r_x.at[h])

        def send_oq(h, i):
            return remote(
                oq.at[peer(i), h], oqin.at[k, h], s_oq, r_oq, (c, peer(i))
            )

        def send_dkv(h, i):
            return remote(
                loc.at[peer(i), h], dkvin.at[k, h], s_dkv, r_dkv, (c, peer(i))
            )

        def aside(h, ox, oz):
            rs, xb = flat[h][3:5]
            return remote(rs.at[oz, ox], xb.at[oz, ox], s_y.at[h], r_y.at[h, oz], (at(-ox, 0), k))

        def gathered(h, oz):
            drain(flat[h][4].at[oz, pl.ds(1, nx - 1)], r_y.at[h, oz])

        def outputs(h):
            g, rs, xb = flat[h][2:5]
            for oz in (4, 3, 5, 2, 6, 1, 7, 0):
                for ox in range(1, nx):
                    rs[oz, ox] = g[rof[at(-ox, -oz)]]
                    aside(h, ox, oz).start()
                if oz > 0:
                    xb[oz, 0] = g[rof[at(0, -oz)]]

            @pl.loop(1, nh)
            def _(i):
                send_oq(h, i).start()

            oqin[k, h] = oq[k, h]

        def toward(s, dist):
            return (-step[s] * dist) % nz

        def back(h, s, stage, b):
            b4, b3, b2, b1, m2, m1 = backs[h][s]
            xb = flat[h][4]
            first = far[1 - s][0]
            src, dst = (
                (xb.at[4, pl.ds(first, 2)], b4),
                (xb.at[toward(s, 3)], b3.at[pl.ds(0, 4)]),
                (b4, b3.at[pl.ds(4, 2)]),
                (m2.at[b], b2.at[b]),
                (m1.at[b], b1.at[b]),
            )[stage]
            rsem = r_g.at[h, s, stage] if stage < 3 else r_b.at[h, s, stage - 3, b]
            return remote(src, dst, s_g.at[h, s], rsem, (at(0, step[s]), k))

        def back_start(h):
            gathered(h, 4)
            for s in range(2):
                back(h, s, 0, 0).start()
            for s in range(2):
                gathered(h, toward(s, 3))
                back(h, s, 1, 0).start()
            for s in range(2):
                back(h, s, 0, 0).wait_recv()
                back(h, s, 2, 0).start()

        def back_two(h):
            xb = flat[h][4]
            for s in range(2):
                gathered(h, toward(s, 2))
                back(h, s, 1, 0).wait_recv()
                back(h, s, 2, 0).wait_recv()

            @pl.loop(1, nh + 1)
            def _(i):
                b = peer(i)
                for s in range(2):
                    b3, m2 = backs[h][s][1], backs[h][s][4]
                    oz = toward(s, 2)
                    src = at(0, 2 * step[s])
                    acc = jnp.zeros((pair, BLOCK), jnp.float32)
                    for ox in range(nx):
                        acc = acc + xb[oz, ox] * is_block(src, at(ox, 0), b)
                        acc = acc + b3[ox] * is_block(src, at(ox, -step[s]), b)
                    for n, ox in enumerate(far[1 - s]):
                        acc = acc + b3[4 + n] * is_block(src, at(ox, -2 * step[s]), b)
                    m2[b] = acc
                    back(h, s, 3, b).start()

        def back_one(h, first=1, last=nh + 1):
            xb = flat[h][4]
            if first == 1:
                for s in range(2):
                    gathered(h, toward(s, 1))

            @pl.loop(first, last)
            def _(i):
                b = peer(i)
                for s in range(2):
                    b2, m1 = backs[h][s][2], backs[h][s][5]
                    oz = toward(s, 1)
                    src = at(0, step[s])
                    back(h, s, 3, b).wait_recv()
                    acc = b2[b]
                    for ox in range(nx):
                        acc = acc + xb[oz, ox] * is_block(src, at(ox, 0), b)
                    m1[b] = acc
                    back(h, s, 4, b).start()

        def back_done(h):
            xb = flat[h][4]
            gathered(h, 0)

            def total(b):
                for s in range(2):
                    back(h, s, 4, b).wait_recv()
                acc = loc[b, h] + backs[h][0][3][b] + backs[h][1][3][b]
                for ox in range(1, nx):
                    acc = acc + xb[0, ox] * is_block(c, at(ox, 0), b)
                return acc

            @pl.loop(1, nh)
            def _(i):
                loc[peer(i), h] = total(peer(i))
                send_dkv(h, i).start()

            dkvin[k, h] = total(k)

        def table_head(i):
            return remote(
                tl.at[pl.ds(peer(i) * share, share)], trs.at[k], s_ta, r_ta, (c, peer(i))
            )

        def table_x(ox):
            return remote(tx.at[(x + ox) % nx], txin.at[x], s_tx, r_tx, (at(ox, 0), k))

        def table_z(oz):
            return remote(tb.at[(z + oz) % nz], tbin.at[z], s_tb, r_tb, (at(0, oz), k))

        def gather_z(oz):
            return remote(tc.at[z], tc.at[z], s_tc, r_tc, (at(0, oz), k))

        def gather_x(ox):
            return remote(tg.at[x], tg.at[x], s_tg, r_tg, (at(ox, 0), k))

        mate = 2 * (k // 2) + 1 - k % 2

        def table_y(i):
            part = table_out.at[pl.ds(k * share, share)]
            return remote(tsum, part, s_td, r_td.at[i], (c, (k + 2 * i) % nh))

        def table_mate(src, j):
            return remote(src, table_out.at[pl.ds(j * share, share)], s_td, r_tm, (c, mate))

        def table_first():
            @pl.loop(0, nbias)
            def _(t):
                acc = jnp.zeros((BLOCK, BLOCK), jnp.float32)
                for r in range(blocks * (NEI + 1)):
                    acc = acc + ds[r] * (bidx[r] == t).astype(jnp.float32)
                tl[t] = acc

            @pl.loop(1, nh)
            def _(i):
                table_head(i).start()

            trs[k] = tl[pl.ds(k * share, share)]

        def table_second():
            mine = jnp.concatenate(
                [jnp.sum(gacc[h], axis=0, keepdims=True) for h in range(HEADS)]
                + [jnp.zeros((8 - HEADS, BLOCK), jnp.float32)],
                axis=0,
            )
            drain(trs.at[pl.ds(0, nh - 1)], r_ta)
            for t in range(nx):
                rows = pl.ds(t * quarter % BLOCK, quarter)
                acc = trs[0, t * quarter // BLOCK, rows, :]
                for i in range(1, nh):
                    acc = acc + trs[i, t * quarter // BLOCK, rows, :]
                tx[t, 0:quarter, :] = acc
                tx[t, quarter : quarter + 8, :] = mine
            for ox in range(1, nx):
                table_x(ox).start()
            txin[x] = tx[x]

        def table_third():
            drain(txin.at[pl.ds(0, nx - 1)], r_tx)
            acc = txin[0]
            for i in range(1, nx):
                acc = acc + txin[i]
            for t in range(nz):
                tb[t, 0:piece, :] = acc[t * piece : (t + 1) * piece]
                tb[t, piece : piece + 8, :] = acc[quarter:]
            for oz in range(1, nz):
                table_z(oz).start()
            tbin[z] = tb[z]

        def table_fourth():
            drain(tbin.at[pl.ds(0, nz - 1)], r_tb)
            acc = tbin[0]
            for i in range(1, nz):
                acc = acc + tbin[i]
            tc[z] = acc[0:piece]
            gain_out[...] = acc[piece : piece + 8]
            for oz in range(1, nz):
                gather_z(oz).start()

        def table_fifth():
            drain(tc.at[pl.ds(0, nz - 1)], r_tc)
            tg[x] = tc[...].reshape(quarter, BLOCK)
            for ox in range(1, nx):
                gather_x(ox).start()

        def table_sixth():
            drain(tg.at[pl.ds(0, nx - 1)], r_tg)
            for t in range(nx):
                tsum[t * quarter // BLOCK, pl.ds(t * quarter % BLOCK, quarter), :] = tg[t]
            for i in range(1, nh // 2):
                table_y(i).start()
            table_mate(tsum, k).start()
            table_out[pl.ds(k * share, share)] = tsum[...]

        def table_last():
            for i in range(1, nh // 2):
                j = (k + nh - 2 * i) % nh
                part = table_out.at[pl.ds(j * share, share)]
                drain(part, r_td.at[i])
                table_mate(part, j).start()

        def restore(src, first, second):
            for n, ref in enumerate((first, second)):
                rows = []
                for j in range(nh):
                    for h in range(HEADS):
                        rows.append(src[j, h, n * dim : (n + 1) * dim, :])
                ref[...] = jnp.transpose(jnp.concatenate(rows, axis=0))

        arrived(0)
        compute(0, 0, 3)
        hop_three(1)
        compute(0, 3, 6)
        hop_four(1)
        compute(0, 6, blocks)
        hop_last(1)
        outputs(0)
        arrived(1)
        compute(1, 0, 2)
        back_start(0)
        compute(1, 2, 4)
        back_two(0)
        compute(1, 4, 7)
        back_one(0)
        compute(1, 7, blocks)
        outputs(1)
        table_first()
        back_start(1)
        back_done(0)
        back_two(1)
        table_second()
        table_third()
        back_one(1, 1, 5)
        table_fourth()
        back_one(1, 5)
        table_fifth()
        table_sixth()
        drain(oqin.at[pl.ds(0, nh - 1)], r_oq)
        restore(oqin, o_out, dq_out)
        back_done(1)
        table_last()
        drain(dkvin.at[pl.ds(0, nh - 1)], r_dkv)
        restore(dkvin, dk_out, dv_out)
        drain(table_out.at[pl.ds(0, nbias // 2)], r_tm)
        for sem in (s_kv, s_qd, s_oq, s_dkv):
            drain(oqin.at[pl.ds(0, nh - 1)], sem)
        for sem in (s_ta, s_td):
            drain(trs.at[pl.ds(0, nh - 1)], sem)
        drain(txin.at[pl.ds(0, nx - 1)], s_tx)
        drain(tbin.at[pl.ds(0, nz - 1)], s_tb)
        drain(tc.at[pl.ds(0, nz - 1)], s_tc)
        drain(tg.at[pl.ds(0, nx - 1)], s_tg)
        for h in range(HEADS):
            for sem in (s_x.at[h], s_y.at[h], s_f.at[h, 0], s_f.at[h, 1], s_g.at[h, 0], s_g.at[h, 1]):
                drain(flat[h][0].at[pl.ds(0, 3 * nz)], sem)

    def f32(*shape):
        return pltpu.VMEM(shape, jnp.float32)

    def sems(*shape):
        return pltpu.SemaphoreType.DMA(shape)

    one = pltpu.SemaphoreType.DMA
    scratch = (
        [f32(BLOCK, nh * width)] * 4
        + [f32(nbias, BLOCK, BLOCK), sems(5)]
        + [f32(nh, HEADS, pair, BLOCK)] * 2
        + [f32(nh, pair, BLOCK)] * 2
        + [f32(nh, HEADS, pair, BLOCK)] * 5
        + [f32(blocks * (NEI + 1), BLOCK, BLOCK), f32(HEADS, 8, BLOCK)]
        + [f32(nbias, BLOCK, BLOCK), f32(nh, share, BLOCK, BLOCK), f32(share, BLOCK, BLOCK)]
        + [f32(nx, quarter + 8, BLOCK)] * 2
        + [f32(nz, piece + 8, BLOCK)] * 2
        + [f32(nz, piece, BLOCK), f32(nx, quarter, BLOCK)]
        + [one, sems(HEADS, nh)]
        + [one] * 18
        + [sems(nh // 2)]
        + [sems(HEADS, 2), sems(HEADS, 2, nh), sems(HEADS, 2, 4)]
        + [sems(HEADS)] * 2
        + [sems(HEADS, 2), sems(HEADS, 2, 3), sems(HEADS, 2, 2, nh)]
        + [sems(HEADS), sems(HEADS, nz)]
        + [f32(n, pair, BLOCK) for n in (blocks, blocks, 6, 2, 6)] * (2 * HEADS)
        + [f32(n, pair, BLOCK) for n in (2, 6, blocks, blocks, blocks, blocks)] * (2 * HEADS)
        + [
            f32(nc, pair, BLOCK),
            f32(nc, pair, BLOCK),
            f32(requests, pair, BLOCK),
            f32(nz, nx, pair, BLOCK),
            f32(nz, nx, pair, BLOCK),
        ]
        * HEADS
    )
    return kernel, scratch


def solution(mesh):
    nc = mesh.shape["ctx"]
    nh = mesh.shape["head"]
    nx = 4
    nz = nc // nx

    def body(queries, keys, values, grad_out, neighbours, bias_index, bias_table, head_gain):
        rows, columns = queries.shape
        nbias = bias_table.shape[0]
        dim = columns // (nh * HEADS)
        blocks = nh
        requests = blocks * NEI
        me = lax.axis_index("ctx")
        asks = neighbours.reshape(nc, requests)
        owner = asks // blocks
        local = asks % blocks
        match = owner[None, :, :] == jnp.arange(nc)[:, None, None]
        key = jnp.max(jnp.where(match, local[None, :, :], -1), axis=2)
        own = lax.dynamic_index_in_dim(asks, me, 0, keepdims=False)
        wanted = (own // blocks)[None, :] == jnp.arange(nc)[:, None]
        rof = jnp.max(jnp.where(wanted, jnp.arange(requests)[None, :], 0), axis=1)
        kernel, scratch = make_kernel(nx, nz, nh, nbias, dim)
        smem = pl.BlockSpec(memory_space=pltpu.SMEM)
        vmem = pl.BlockSpec(memory_space=pltpu.VMEM)
        wide = jax.ShapeDtypeStruct((rows, columns), jnp.float32)
        outs = pl.pallas_call(
            kernel,
            out_shape=[wide] * 4
            + [
                jax.ShapeDtypeStruct(bias_table.shape, jnp.float32),
                jax.ShapeDtypeStruct((8, BLOCK), jnp.float32),
            ],
            in_specs=[smem] * 5 + [pl.BlockSpec(memory_space=pltpu.HBM)] * 5,
            out_specs=[vmem] * 6,
            scratch_shapes=scratch,
            compiler_params=pltpu.CompilerParams(
                collective_id=0, has_side_effects=True, vmem_limit_bytes=52 * 1024 * 1024
            ),
        )(
            key.reshape(-1), rof, own, bias_index.reshape(-1), head_gain,
            queries, keys, values, grad_out, bias_table,
        )
        def store(*refs):
            ins, dst, sem = refs[:6], refs[6:12], refs[12]
            copies = [pltpu.make_async_copy(ins[n], dst[n], sem.at[n]) for n in range(5)]
            for copy in copies:
                copy.start()
            for h in range(HEADS):
                dst[5][h] = jnp.sum(ins[5][h : h + 1, :])
            for copy in copies:
                copy.wait()

        return pl.pallas_call(
            store,
            out_shape=[wide] * 4
            + [
                jax.ShapeDtypeStruct(bias_table.shape, jnp.float32),
                jax.ShapeDtypeStruct((HEADS,), jnp.float32),
            ],
            in_specs=[vmem] * 6,
            out_specs=[pl.BlockSpec(memory_space=pl.ANY)] * 5 + [smem],
            scratch_shapes=[pltpu.SemaphoreType.DMA((5,))],
            compiler_params=pltpu.CompilerParams(vmem_limit_bytes=8 * 1024 * 1024),
        )(*outs)

    return jax.shard_map(
        body,
        mesh=mesh,
        in_specs=(
            P(("ctx", "head"), None),
            P(("ctx", "head"), None),
            P(("ctx", "head"), None),
            P(("ctx", "head"), None),
            P(),
            P("ctx", None),
            P(),
            P("head"),
        ),
        out_specs=(
            P(("ctx", "head"), None),
            P(("ctx", "head"), None),
            P(("ctx", "head"), None),
            P(("ctx", "head"), None),
            P(),
            P("head"),
        ),
        check_vma=False,
    )
```

```python
import jax
import jax.numpy as jnp
from jax import lax
from jax.experimental import pallas as pl
from jax.experimental.pallas import tpu as pltpu
from jax.sharding import PartitionSpec as P

BLOCK = 128
NEI = 2
HEADS = 2
MESH = pl.DeviceIdType.MESH
HIGHEST = lax.Precision.HIGHEST


def mm(a, b, ca, cb):
    return lax.dot_general(
        a, b, (((ca,), (cb,)), ((), ())), precision=HIGHEST, preferred_element_type=jnp.float32
    )


def make_kernel(nx, nz, nh, nbias, dim):
    nc = nx * nz
    blocks = nh
    requests = blocks * NEI
    pair = 2 * dim
    width = HEADS * dim
    share = nbias // nh
    piece = share * BLOCK // nc
    quarter = share * BLOCK // nx
    factor = dim ** (-0.5)

    def kernel(
        key, rof, nbr, bidx, gain,
        q_hbm, k_hbm, v_hbm, g_hbm, table_hbm,
        o_out, dq_out, dk_out, dv_out, table_out, gain_out,
        q_in, k_in, v_in, g_in, table, s_in,
        tkv, tqd, kv0, kv1, qd, loc, oq, oqin, dkvin,
        ds, gacc, tl, trs, tsum, tx, txin, tb, tbin, tc, tg,
        s_kv, r_kv, s_qd, r_qd, s_oq, r_oq, s_dkv, r_dkv,
        s_ta, r_ta, s_tx, r_tx, s_tb, r_tb, s_tc, r_tc, s_tg, r_tg, s_td, r_tm, r_td,
        s_f, r_f, r_h, s_x, r_x, s_g, r_g, r_b, s_y, r_y,
        *rest,
    ):
        kv = (kv0, kv1)
        hops = [[rest[(h * 2 + s) * 5 : (h * 2 + s) * 5 + 5] for s in range(2)] for h in range(HEADS)]
        rest = rest[HEADS * 10 :]
        backs = [[rest[(h * 2 + s) * 6 : (h * 2 + s) * 6 + 6] for s in range(2)] for h in range(HEADS)]
        rest = rest[HEADS * 12 :]
        flat = [rest[h * 5 : h * 5 + 5] for h in range(HEADS)]

        c = lax.axis_index("ctx")
        k = lax.axis_index("head")
        x = c // nz
        z = c % nz

        def at(dx, dz):
            return ((x + nx + dx) % nx) * nz + (z + nz + dz) % nz

        def peer(i):
            return (k + i) % nh

        def wants(src, dst):
            return key[src * nc + dst]

        def pick(src, dst):
            return jnp.maximum(wants(src, dst), 0)

        def is_block(src, dst, b):
            return (wants(src, dst) == b).astype(jnp.float32)

        def remote(src, dst, ssem, rsem, dev):
            return pltpu.make_async_remote_copy(
                src, dst, ssem, rsem, device_id=dev, device_id_type=MESH
            )

        inputs = [
            pltpu.make_async_copy(src, dst, s_in.at[n])
            for n, (src, dst) in enumerate(
                (
                    (k_hbm, k_in), (v_hbm, v_in), (q_hbm, q_in), (g_hbm, g_in), (table_hbm, table)
                )
            )
        ]
        for copy in inputs:
            copy.start()

        barrier = pltpu.get_barrier_semaphore()

        @pl.loop(1, nh)
        def _(i):
            pl.semaphore_signal(barrier, inc=1, device_id=(c, peer(i)), device_id_type=MESH)

        near = [at(ox, 0) for ox in range(1, nx)] + [at(0, 1), at(0, -1)]
        for d in near:
            pl.semaphore_signal(barrier, inc=1, device_id=(d, k), device_id_type=MESH)

        def drain(ref, sem):
            pltpu.make_async_copy(ref, ref, sem).wait()

        def turn(first, second, dst):
            for n, ref in enumerate((first, second)):
                full = jnp.transpose(ref[...])
                for j in range(nh):
                    for h in range(HEADS):
                        row = j * width + h * dim
                        dst[j, h, n * dim : (n + 1) * dim, :] = full[row : row + dim, :]

        def to_head(src, dst, ssem, rsem, i):
            return remote(src.at[peer(i)], dst.at[k], ssem, rsem, (c, peer(i)))

        def kv_head(h, i):
            return remote(
                tkv.at[peer(i), h], kv[h].at[k], s_kv, r_kv.at[h, i], (c, peer(i))
            )

        inputs[0].wait()
        inputs[1].wait()
        turn(k_in, v_in, tkv)
        pl.semaphore_wait(barrier, nh - 1 + len(near))
        for h in range(HEADS):

            @pl.loop(1, nh)
            def _(i):
                kv_head(h, i).start()

        for h in range(HEADS):
            kv[h][k] = tkv[k, h]

        step = (1, -1)
        far = ((0, 1), (2, 3))

        def origin(i):
            return (k + nh - i) % nh

        def forward(h, s, stage, i):
            a1, a2, a3, a4, t3 = hops[h][s]
            src, dst = (
                (kv[h].at[origin(i)], a1.at[origin(i)]),
                (a1.at[origin(i)], a2.at[origin(i)]),
                (t3.at[pl.ds(4, 2)], a3.at[pl.ds(4, 2)]),
                (t3.at[pl.ds(0, 4)], a3.at[pl.ds(0, 4)]),
                (a3.at[pl.ds(4, 2)], a4),
            )[stage]
            rsem = r_f.at[h, s, i] if stage == 0 else r_h.at[h, s, stage - 1]
            return remote(src, dst, s_f.at[h, s], rsem, (at(0, step[s]), k))

        def across(h, src, ox, oz):
            o = ox * nz + oz
            return remote(src, flat[h][0].at[o], s_x.at[h], r_x.at[h], (at(ox, 0), k))

        def deliver(h, s, dist):
            arr, xs = flat[h][:2]
            oz = (step[s] * dist) % nz
            src = at(0, -step[s] * dist)
            buf = hops[h][s][dist - 1]
            if dist <= 2:
                for ox in range(1, nx):
                    xs[ox * nz + oz] = buf[pick(src, at(ox, 0))]
                    across(h, xs.at[ox * nz + oz], ox, oz).start()
                arr[oz] = buf[pick(src, c)]
            else:
                for n, ox in enumerate(range(nx) if dist == 3 else far[s]):
                    if ox == 0:
                        arr[oz] = buf[n]
                    else:
                        across(h, buf.at[n], ox, oz).start()

        def hop_one(h, first, last):
            @pl.loop(first, last)
            def _(i):
                kv_head(h, i).wait_recv()
                for s in range(2):
                    forward(h, s, 0, i).start()

        def hop_own(h):
            for s in range(2):
                forward(h, s, 0, 0).start()

        def row(h):
            for ox in range(1, nx):
                flat[h][1][ox * nz] = kv[h][pick(c, at(ox, 0))]
                across(h, flat[h][1].at[ox * nz], ox, 0).start()

        def hop_two(h):
            @pl.loop(0, nh)
            def _(i):
                for s in range(2):
                    forward(h, s, 0, i).wait_recv()
                    forward(h, s, 1, i).start()

            for s in range(2):
                deliver(h, s, 1)

        def hop_three(h):
            for s in range(2):

                a2, t3 = hops[h][s][1], hops[h][s][4]
                drain(a2, r_h.at[h, s, 0])
                src = at(0, -2 * step[s])
                for n, ox in enumerate(far[s]):
                    t3[nx + n] = a2[pick(src, at(ox, 2 * step[s]))]
                forward(h, s, 2, 0).start()
                for ox in range(nx):
                    t3[ox] = a2[pick(src, at(ox, step[s]))]
                forward(h, s, 3, 0).start()
            for s in range(2):
                deliver(h, s, 2)

        def hop_four(h):
            for s in range(2):
                forward(h, s, 2, 0).wait_recv()
                forward(h, s, 4, 0).start()
            for s in range(2):
                forward(h, s, 3, 0).wait_recv()
                deliver(h, s, 3)

        def hop_last(h):
            for s in range(2):
                forward(h, s, 4, 0).wait_recv()
                deliver(h, s, 4)

        hop_own(0)
        inputs[2].wait()
        inputs[3].wait()
        turn(q_in, g_in, tqd)
        hop_one(0, 1, nh)

        @pl.loop(1, nh)
        def _(i):
            to_head(tqd, qd, s_qd, r_qd, i).start()

        qd[k] = tqd[k]
        row(0)
        hop_two(0)
        hop_own(1)
        hop_one(1, 1, 4)
        hop_three(0)
        hop_one(1, 4, nh)
        row(1)
        hop_four(0)
        hop_two(1)
        hop_last(0)

        drain(qd.at[pl.ds(0, nh - 1)], r_qd)

        inputs[4].wait()
        gacc[...] = jnp.zeros_like(gacc)

        def attend(b, h):
            arr, g = flat[h][0], flat[h][2]
            gain_h = gain[h]
            qt = qd[b, h, 0:dim, :] * factor
            dot = qd[b, h, dim:pair, :]
            q = jnp.transpose(qt)
            do = jnp.transpose(dot)
            sets = [kv[h][b]]
            for m in range(NEI):
                owner = nbr[b * NEI + m] // blocks
                ox = (x + nx - owner // nz) % nx
                oz = (z + nz - owner % nz) % nz
                sets.append(arr[ox * nz + oz])
            bias = [table[bidx[b * (NEI + 1) + m]] for m in range(NEI + 1)]
            scores = [mm(q, t[0:dim], 1, 0) + gain_h * e for t, e in zip(sets, bias)]
            top = jnp.max(scores[0], axis=1, keepdims=True)
            for s in scores[1:]:
                top = jnp.maximum(top, jnp.max(s, axis=1, keepdims=True))
            weights = [jnp.exp(s - top) for s in scores]
            total = sum(jnp.sum(w, axis=1, keepdims=True) for w in weights)
            inverse = 1.0 / total
            weights = [w * inverse for w in weights]
            wgrad = [mm(do, t[dim:pair], 1, 0) for t in sets]
            delta = sum(jnp.sum(w * d, axis=1, keepdims=True) for w, d in zip(weights, wgrad))
            sgrad = [w * (d - delta) for w, d in zip(weights, wgrad)]
            oq[b, h, 0:dim, :] = sum(mm(t[dim:pair], w, 1, 1) for t, w in zip(sets, weights))
            oq[b, h, dim:pair, :] = factor * sum(mm(t[0:dim], s, 1, 1) for t, s in zip(sets, sgrad))
            part = jnp.zeros((8, BLOCK), jnp.float32)
            for m in range(NEI + 1):
                dk = mm(qt, sgrad[m], 1, 0)
                dv = mm(dot, weights[m], 1, 0)
                if m == 0:
                    loc[b, h, 0:dim, :] = dk
                    loc[b, h, dim:pair, :] = dv
                else:
                    g[b * NEI + m - 1, 0:dim, :] = dk
                    g[b * NEI + m - 1, dim:pair, :] = dv
                scaled = gain_h * sgrad[m]
                if h == 0:
                    ds[b * (NEI + 1) + m] = scaled
                else:
                    ds[b * (NEI + 1) + m] += scaled
                prod = sgrad[m] * bias[m]
                part = part + jnp.sum(prod.reshape(BLOCK // 8, 8, BLOCK), axis=0)
            gacc[h] += part

        def compute(h, first, last):
            @pl.loop(first, last)
            def _(b):
                attend(b, h)

        def arrived(h):
            drain(flat[h][0].at[pl.ds(nz, nc - nz)], r_x.at[h])

        def send_oq(h, i):
            return remote(
                oq.at[peer(i), h], oqin.at[k, h], s_oq, r_oq, (c, peer(i))
            )

        def send_dkv(h, i):
            return remote(
                loc.at[peer(i), h], dkvin.at[k, h], s_dkv, r_dkv, (c, peer(i))
            )

        def aside(h, ox, oz):
            rs, xb = flat[h][3:5]
            return remote(rs.at[oz, ox], xb.at[oz, ox], s_y.at[h], r_y.at[h, oz], (at(-ox, 0), k))

        def gathered(h, oz):
            drain(flat[h][4].at[oz, pl.ds(1, nx - 1)], r_y.at[h, oz])

        def outputs(h):
            g, rs, xb = flat[h][2:5]
            for oz in (4, 3, 5, 2, 6, 1, 7, 0):
                for ox in range(1, nx):
                    rs[oz, ox] = g[rof[at(-ox, -oz)]]
                    aside(h, ox, oz).start()
                if oz > 0:
                    xb[oz, 0] = g[rof[at(0, -oz)]]

            @pl.loop(1, nh)
            def _(i):
                send_oq(h, i).start()

            oqin[k, h] = oq[k, h]

        def toward(s, dist):
            return (-step[s] * dist) % nz

        def back(h, s, stage, b):
            b4, b3, b2, b1, m2, m1 = backs[h][s]
            xb = flat[h][4]
            first = far[1 - s][0]
            src, dst = (
                (xb.at[4, pl.ds(first, 2)], b4),
                (xb.at[toward(s, 3)], b3.at[pl.ds(0, 4)]),
                (b4, b3.at[pl.ds(4, 2)]),
                (m2.at[b], b2.at[b]),
                (m1.at[b], b1.at[b]),
            )[stage]
            rsem = r_g.at[h, s, stage] if stage < 3 else r_b.at[h, s, stage - 3, b]
            return remote(src, dst, s_g.at[h, s], rsem, (at(0, step[s]), k))

        def back_start(h):
            gathered(h, 4)
            for s in range(2):
                back(h, s, 0, 0).start()
            for s in range(2):
                gathered(h, toward(s, 3))
                back(h, s, 1, 0).start()
            for s in range(2):
                back(h, s, 0, 0).wait_recv()
                back(h, s, 2, 0).start()

        def back_two(h):
            xb = flat[h][4]
            for s in range(2):
                gathered(h, toward(s, 2))
                back(h, s, 1, 0).wait_recv()
                back(h, s, 2, 0).wait_recv()

            @pl.loop(1, nh + 1)
            def _(i):
                b = peer(i)
                for s in range(2):
                    b3, m2 = backs[h][s][1], backs[h][s][4]
                    oz = toward(s, 2)
                    src = at(0, 2 * step[s])
                    acc = jnp.zeros((pair, BLOCK), jnp.float32)
                    for ox in range(nx):
                        acc = acc + xb[oz, ox] * is_block(src, at(ox, 0), b)
                        acc = acc + b3[ox] * is_block(src, at(ox, -step[s]), b)
                    for n, ox in enumerate(far[1 - s]):
                        acc = acc + b3[4 + n] * is_block(src, at(ox, -2 * step[s]), b)
                    m2[b] = acc
                    back(h, s, 3, b).start()

        def back_one(h, first=1, last=nh + 1):
            xb = flat[h][4]
            if first == 1:
                for s in range(2):
                    gathered(h, toward(s, 1))

            @pl.loop(first, last)
            def _(i):
                b = peer(i)
                for s in range(2):
                    b2, m1 = backs[h][s][2], backs[h][s][5]
                    oz = toward(s, 1)
                    src = at(0, step[s])
                    back(h, s, 3, b).wait_recv()
                    acc = b2[b]
                    for ox in range(nx):
                        acc = acc + xb[oz, ox] * is_block(src, at(ox, 0), b)
                    m1[b] = acc
                    back(h, s, 4, b).start()

        def back_done(h):
            xb = flat[h][4]
            gathered(h, 0)

            def total(b):
                for s in range(2):
                    back(h, s, 4, b).wait_recv()
                acc = loc[b, h] + backs[h][0][3][b] + backs[h][1][3][b]
                for ox in range(1, nx):
                    acc = acc + xb[0, ox] * is_block(c, at(ox, 0), b)
                return acc

            @pl.loop(1, nh)
            def _(i):
                loc[peer(i), h] = total(peer(i))
                send_dkv(h, i).start()

            dkvin[k, h] = total(k)

        def table_head(i):
            return remote(
                tl.at[pl.ds(peer(i) * share, share)], trs.at[k], s_ta, r_ta, (c, peer(i))
            )

        def table_x(ox):
            return remote(tx.at[(x + ox) % nx], txin.at[x], s_tx, r_tx, (at(ox, 0), k))

        def table_z(oz):
            return remote(tb.at[(z + oz) % nz], tbin.at[z], s_tb, r_tb, (at(0, oz), k))

        def gather_z(oz):
            return remote(tc.at[z], tc.at[z], s_tc, r_tc, (at(0, oz), k))

        def gather_x(ox):
            return remote(tg.at[x], tg.at[x], s_tg, r_tg, (at(ox, 0), k))

        mate = 2 * (k // 2) + 1 - k % 2

        def table_y(i):
            part = table_out.at[pl.ds(k * share, share)]
            return remote(tsum, part, s_td, r_td.at[i], (c, (k + 2 * i) % nh))

        def table_mate(src, j):
            return remote(src, table_out.at[pl.ds(j * share, share)], s_td, r_tm, (c, mate))

        def table_first():
            @pl.loop(0, nbias)
            def _(t):
                acc = jnp.zeros((BLOCK, BLOCK), jnp.float32)
                for r in range(blocks * (NEI + 1)):
                    acc = acc + ds[r] * (bidx[r] == t).astype(jnp.float32)
                tl[t] = acc

            @pl.loop(1, nh)
            def _(i):
                table_head(i).start()

            trs[k] = tl[pl.ds(k * share, share)]

        def table_second():
            mine = jnp.concatenate(
                [jnp.sum(gacc[h], axis=0, keepdims=True) for h in range(HEADS)]
                + [jnp.zeros((8 - HEADS, BLOCK), jnp.float32)],
                axis=0,
            )
            drain(trs.at[pl.ds(0, nh - 1)], r_ta)
            for t in range(nx):
                rows = pl.ds(t * quarter % BLOCK, quarter)
                acc = trs[0, t * quarter // BLOCK, rows, :]
                for i in range(1, nh):
                    acc = acc + trs[i, t * quarter // BLOCK, rows, :]
                tx[t, 0:quarter, :] = acc
                tx[t, quarter : quarter + 8, :] = mine
            for ox in range(1, nx):
                table_x(ox).start()
            txin[x] = tx[x]

        def table_third():
            drain(txin.at[pl.ds(0, nx - 1)], r_tx)
            acc = txin[0]
            for i in range(1, nx):
                acc = acc + txin[i]
            for t in range(nz):
                tb[t, 0:piece, :] = acc[t * piece : (t + 1) * piece]
                tb[t, piece : piece + 8, :] = acc[quarter:]
            for oz in range(1, nz):
                table_z(oz).start()
            tbin[z] = tb[z]

        def table_fourth():
            drain(tbin.at[pl.ds(0, nz - 1)], r_tb)
            acc = tbin[0]
            for i in range(1, nz):
                acc = acc + tbin[i]
            tc[z] = acc[0:piece]
            gain_out[...] = acc[piece : piece + 8]
            for oz in range(1, nz):
                gather_z(oz).start()

        def table_fifth():
            drain(tc.at[pl.ds(0, nz - 1)], r_tc)
            tg[x] = tc[...].reshape(quarter, BLOCK)
            for ox in range(1, nx):
                gather_x(ox).start()

        def table_sixth():
            drain(tg.at[pl.ds(0, nx - 1)], r_tg)
            for t in range(nx):
                tsum[t * quarter // BLOCK, pl.ds(t * quarter % BLOCK, quarter), :] = tg[t]
            for i in range(1, nh // 2):
                table_y(i).start()
            table_mate(tsum, k).start()
            table_out[pl.ds(k * share, share)] = tsum[...]

        def table_last():
            for i in range(1, nh // 2):
                j = (k + nh - 2 * i) % nh
                part = table_out.at[pl.ds(j * share, share)]
                drain(part, r_td.at[i])
                table_mate(part, j).start()

        def restore(src, first, second):
            for n, ref in enumerate((first, second)):
                rows = []
                for j in range(nh):
                    for h in range(HEADS):
                        rows.append(src[j, h, n * dim : (n + 1) * dim, :])
                ref[...] = jnp.transpose(jnp.concatenate(rows, axis=0))

        arrived(0)
        compute(0, 0, 3)
        hop_three(1)
        compute(0, 3, 6)
        hop_four(1)
        compute(0, 6, blocks)
        hop_last(1)
        outputs(0)
        arrived(1)
        compute(1, 0, 2)
        back_start(0)
        compute(1, 2, 4)
        back_two(0)
        compute(1, 4, 7)
        back_one(0)
        compute(1, 7, blocks)
        outputs(1)
        table_first()
        back_start(1)
        back_done(0)
        back_two(1)
        table_second()
        table_third()
        back_one(1, 1, 5)
        table_fourth()
        back_one(1, 5)
        drain(oqin.at[pl.ds(0, nh - 1)], r_oq)
        restore(oqin, o_out, dq_out)
        table_fifth()
        table_sixth()
        back_done(1)
        table_last()
        drain(dkvin.at[pl.ds(0, nh - 1)], r_dkv)
        restore(dkvin, dk_out, dv_out)
        drain(table_out.at[pl.ds(0, nbias // 2)], r_tm)
        for sem in (s_kv, s_qd, s_oq, s_dkv):
            drain(oqin.at[pl.ds(0, nh - 1)], sem)
        for sem in (s_ta, s_td):
            drain(trs.at[pl.ds(0, nh - 1)], sem)
        drain(txin.at[pl.ds(0, nx - 1)], s_tx)
        drain(tbin.at[pl.ds(0, nz - 1)], s_tb)
        drain(tc.at[pl.ds(0, nz - 1)], s_tc)
        drain(tg.at[pl.ds(0, nx - 1)], s_tg)
        for h in range(HEADS):
            for sem in (s_x.at[h], s_y.at[h], s_f.at[h, 0], s_f.at[h, 1], s_g.at[h, 0], s_g.at[h, 1]):
                drain(flat[h][0].at[pl.ds(0, 3 * nz)], sem)

    def f32(*shape):
        return pltpu.VMEM(shape, jnp.float32)

    def sems(*shape):
        return pltpu.SemaphoreType.DMA(shape)

    one = pltpu.SemaphoreType.DMA
    scratch = (
        [f32(BLOCK, nh * width)] * 4
        + [f32(nbias, BLOCK, BLOCK), sems(5)]
        + [f32(nh, HEADS, pair, BLOCK)] * 2
        + [f32(nh, pair, BLOCK)] * 2
        + [f32(nh, HEADS, pair, BLOCK)] * 5
        + [f32(blocks * (NEI + 1), BLOCK, BLOCK), f32(HEADS, 8, BLOCK)]
        + [f32(nbias, BLOCK, BLOCK), f32(nh, share, BLOCK, BLOCK), f32(share, BLOCK, BLOCK)]
        + [f32(nx, quarter + 8, BLOCK)] * 2
        + [f32(nz, piece + 8, BLOCK)] * 2
        + [f32(nz, piece, BLOCK), f32(nx, quarter, BLOCK)]
        + [one, sems(HEADS, nh)]
        + [one] * 18
        + [sems(nh // 2)]
        + [sems(HEADS, 2), sems(HEADS, 2, nh), sems(HEADS, 2, 4)]
        + [sems(HEADS)] * 2
        + [sems(HEADS, 2), sems(HEADS, 2, 3), sems(HEADS, 2, 2, nh)]
        + [sems(HEADS), sems(HEADS, nz)]
        + [f32(n, pair, BLOCK) for n in (blocks, blocks, 6, 2, 6)] * (2 * HEADS)
        + [f32(n, pair, BLOCK) for n in (2, 6, blocks, blocks, blocks, blocks)] * (2 * HEADS)
        + [
            f32(nc, pair, BLOCK),
            f32(nc, pair, BLOCK),
            f32(requests, pair, BLOCK),
            f32(nz, nx, pair, BLOCK),
            f32(nz, nx, pair, BLOCK),
        ]
        * HEADS
    )
    return kernel, scratch


def solution(mesh):
    nc = mesh.shape["ctx"]
    nh = mesh.shape["head"]
    nx = 4
    nz = nc // nx

    def body(queries, keys, values, grad_out, neighbours, bias_index, bias_table, head_gain):
        rows, columns = queries.shape
        nbias = bias_table.shape[0]
        dim = columns // (nh * HEADS)
        blocks = nh
        requests = blocks * NEI
        me = lax.axis_index("ctx")
        asks = neighbours.reshape(nc, requests)
        owner = asks // blocks
        local = asks % blocks
        match = owner[None, :, :] == jnp.arange(nc)[:, None, None]
        key = jnp.max(jnp.where(match, local[None, :, :], -1), axis=2)
        own = lax.dynamic_index_in_dim(asks, me, 0, keepdims=False)
        wanted = (own // blocks)[None, :] == jnp.arange(nc)[:, None]
        rof = jnp.max(jnp.where(wanted, jnp.arange(requests)[None, :], 0), axis=1)
        kernel, scratch = make_kernel(nx, nz, nh, nbias, dim)
        smem = pl.BlockSpec(memory_space=pltpu.SMEM)
        vmem = pl.BlockSpec(memory_space=pltpu.VMEM)
        wide = jax.ShapeDtypeStruct((rows, columns), jnp.float32)
        outs = pl.pallas_call(
            kernel,
            out_shape=[wide] * 4
            + [
                jax.ShapeDtypeStruct(bias_table.shape, jnp.float32),
                jax.ShapeDtypeStruct((8, BLOCK), jnp.float32),
            ],
            in_specs=[smem] * 5 + [pl.BlockSpec(memory_space=pltpu.HBM)] * 5,
            out_specs=[vmem] * 6,
            scratch_shapes=scratch,
            compiler_params=pltpu.CompilerParams(
                collective_id=0, has_side_effects=True, vmem_limit_bytes=52 * 1024 * 1024
            ),
        )(
            key.reshape(-1), rof, own, bias_index.reshape(-1), head_gain,
            queries, keys, values, grad_out, bias_table,
        )
        def store(*refs):
            ins, dst, sem = refs[:6], refs[6:12], refs[12]
            copies = [pltpu.make_async_copy(ins[n], dst[n], sem.at[n]) for n in range(5)]
            for copy in copies:
                copy.start()
            for h in range(HEADS):
                dst[5][h] = jnp.sum(ins[5][h : h + 1, :])
            for copy in copies:
                copy.wait()

        return pl.pallas_call(
            store,
            out_shape=[wide] * 4
            + [
                jax.ShapeDtypeStruct(bias_table.shape, jnp.float32),
                jax.ShapeDtypeStruct((HEADS,), jnp.float32),
            ],
            in_specs=[vmem] * 6,
            out_specs=[pl.BlockSpec(memory_space=pl.ANY)] * 5 + [smem],
            scratch_shapes=[pltpu.SemaphoreType.DMA((5,))],
            compiler_params=pltpu.CompilerParams(vmem_limit_bytes=8 * 1024 * 1024),
        )(*outs)

    return jax.shard_map(
        body,
        mesh=mesh,
        in_specs=(
            P(("ctx", "head"), None),
            P(("ctx", "head"), None),
            P(("ctx", "head"), None),
            P(("ctx", "head"), None),
            P(),
            P("ctx", None),
            P(),
            P("head"),
        ),
        out_specs=(
            P(("ctx", "head"), None),
            P(("ctx", "head"), None),
            P(("ctx", "head"), None),
            P(("ctx", "head"), None),
            P(),
            P("head"),
        ),
        check_vma=False,
    )
```
